128 devices in a mesh: role: 4 (over x_hi, core), brick: 32 (over y, x_lo, z).
Axes of the slice: x: 4 (x_hi: 2, x_lo: 2; x = x_hi * 2 + x_lo), y: 4, z: 4, core: 2. Of those that a mesh axis runs over, the one named last changes fastest.
Arguments:
- velocity: float32 [3, 64, 512, 128], P(None, 'role', 'brick'), may hold values from -6 to 6
- first_layer: float32 [1536, 1024], P('brick'), may hold values from -0.15625 to 0.15625
- middle_layer: float32 [1024, 1024], P('brick'), may hold values from -0.1875 to 0.1875
- last_layer: float32 [1536, 1024], P('brick'), may hold values from -0.1875 to 0.1875
- first_moment: float32 [1536, 1024], P('brick'), may hold values from -0.06 to 0.06
- middle_moment: float32 [1024, 1024], P('brick'), may hold values from -0.06 to 0.06
- last_moment: float32 [1536, 1024], P('brick'), may hold values from -0.06 to 0.06
- patch_pick: int32 [16384], P(('role', 'brick')), may hold values from 0 to 63
- target_rows: bfloat16 [16384, 1536], P(('role', 'brick')), may hold values from -6 to 6
Outputs:
- velocity_next: float32 [3, 64, 512, 128], P(None, 'role', 'brick')
- first_updated: float32 [1536, 1024], P('brick', 'role')
- middle_updated: float32 [1024, 1024], P('brick', 'role')
- last_updated: float32 [1536, 1024], P('brick', 'role')
- first_momentum: float32 [1536, 1024], P('brick', 'role')
- middle_momentum: float32 [1024, 1024], P('brick', 'role')
- last_momentum: float32 [1536, 1024], P('brick', 'role')
The draws below stay inside these ranges and needn't reach their ends.
Inputs may be any that keep to these rules, and one draw needn't show every extreme that they name: `patch_pick`: entry q names a cube of the brick of device q // 128 in the order of patches.
All inputs are finite; a program needn't handle non-finite values. Where the reference program divides by a largest or mean magnitude, that divisor is 1e-20 or more.
Results may differ from the reference program's by a relative error of at most 0.019.
Values may be sent and summed in bfloat16 or wider, within the bound.
No kernel may reach another device: no remote copies, remote signals or barrier semaphores. Data moves between devices by JAX's collectives and lax.ppermute only.
A program may use at most 128 MiB of HBM per device.

```python
import jax
import jax.numpy as jnp
from jax import lax

PS = 8
HID = 1024
CX = 16
CY = 16
REF_DEV = 128
F = 1536
NP_DEV = 64
NX = 64
NY = 512
NZ = 128
NREF = 16384
N_ROLE = 4
N_BRICK = 32


def draw_velocity(key, part):
    across = (jnp.arange(NY, dtype=jnp.float32) / NY)[None, None, :, None]
    amplitude = 0.5 + across
    random_part = jnp.clip(jax.random.normal(key, (3, NX, NY, NZ), jnp.float32), -4.0, 4.0)
    return amplitude * random_part


def set_ends(array, own_key, smallest, largest):
    dims = array.shape
    index_at = [jax.random.randint(jax.random.fold_in(own_key, axis), (), 0, dims[axis]) for axis in range(len(dims))]
    array = array.at[tuple(index_at)].set(smallest)
    longest = dims.index(max(dims))
    index_at[longest] = (index_at[longest] + 1) % dims[longest]
    return array.at[tuple(index_at)].set(largest)


def levels(stream_key, shape, split, low, high):
    level = 1.0
    for dim, parts in split:
        draws = jax.random.uniform(jax.random.fold_in(jax.random.fold_in(stream_key, 6), dim), (parts,), jnp.float32, low / len(split), high / len(split))
        level = level * jnp.repeat(jnp.exp(draws), shape[dim] // parts).reshape((-1,) + (1,) * (len(shape) - 1 - dim))
    return level


def scatter_about(key, dims, spread, limit, shards=(), held_as=jnp.bfloat16):
    loudness = levels(key, dims, shards, -0.22, 0.18) if shards else 1.0
    drawn = jax.random.normal(key, dims, jnp.float32) * spread * loudness
    return jnp.minimum(jnp.maximum(drawn, -limit), limit).astype(held_as)


def setup_inputs(seed: int = 0) -> dict:
    streams_of = jax.random.split(jax.random.key(seed), 10)
    velocity = draw_velocity(jax.random.fold_in(streams_of[9], 71), 0)
    first_layer = scatter_about(streams_of[1], (F, HID), F ** -0.5, 0.15625, ((0, 32),), jnp.float32)
    middle_layer = scatter_about(streams_of[2], (HID, HID), HID ** -0.5, 0.1875, ((0, 32),), jnp.float32)
    last_layer = scatter_about(streams_of[3], (F, HID), HID ** -0.5, 0.1875, ((0, 32),), jnp.float32)
    first_moment = scatter_about(streams_of[4], (F, HID), 0.01, 0.06, ((0, 32),), jnp.float32)
    middle_moment = scatter_about(streams_of[5], (HID, HID), 0.01, 0.06, ((0, 32),), jnp.float32)
    last_moment = scatter_about(streams_of[6], (F, HID), 0.01, 0.06, ((0, 32),), jnp.float32)
    patch_pick = set_ends(jax.random.randint(streams_of[7], (NREF,), 0, NP_DEV), jax.random.fold_in(streams_of[7], 1), 0, NP_DEV - 1).astype(jnp.int32)
    target_rows = scatter_about(streams_of[8], (NREF, F), 1.0, 6.0, ((0, 128),))
    return dict(velocity=velocity, first_layer=first_layer, middle_layer=middle_layer, last_layer=last_layer, first_moment=first_moment, middle_moment=middle_moment, last_moment=last_moment, patch_pick=patch_pick, target_rows=target_rows)


weno_eps = 1e-6
courant = 0.3
momentum_keep = 0.9
learn_rate = 0.3


def reconstruct(cell_one, cell_two, cell_three, cell_four, cell_five):
    guess_low = (2.0 * cell_one - 7.0 * cell_two + 11.0 * cell_three) / 6.0
    guess_center = (-cell_two + 5.0 * cell_three + 2.0 * cell_four) / 6.0
    guess_high = (2.0 * cell_three + 5.0 * cell_four - cell_five) / 6.0
    bend_low = cell_one - 2.0 * cell_two + cell_three
    tilt_low = cell_one - 4.0 * cell_two + 3.0 * cell_three
    bend_center = cell_two - 2.0 * cell_three + cell_four
    tilt_center = cell_two - cell_four
    bend_high = cell_three - 2.0 * cell_four + cell_five
    tilt_high = 3.0 * cell_three - 4.0 * cell_four + cell_five
    rough_low = weno_eps + 13.0 / 12.0 * bend_low * bend_low + 0.25 * tilt_low * tilt_low
    central_smoothness = weno_eps + 13.0 / 12.0 * bend_center * bend_center + 0.25 * tilt_center * tilt_center
    rough_high = weno_eps + 13.0 / 12.0 * bend_high * bend_high + 0.25 * tilt_high * tilt_high
    weight_low = 0.1 / (rough_low * rough_low)
    weight_center = 0.6 / (central_smoothness * central_smoothness)
    weight_high = 0.3 / (rough_high * rough_high)
    blended = weight_low * guess_low + weight_center * guess_center + weight_high * guess_high
    return blended / (weight_low + weight_center + weight_high)


def window(source, offset, extent, axis_here):
    return lax.slice_in_dim(source, offset, offset + extent + 1, axis=axis_here)


def divergence(padded_field, sweep_direction, max_speed):
    axis_here = sweep_direction - 1
    extent = padded_field.shape[sweep_direction] - 6
    carried_state = padded_field[sweep_direction - 1]
    results = []
    for component in range(3):
        cell_values = padded_field[component]
        flux_per_cell = carried_state * cell_values
        split_high = 0.5 * (flux_per_cell + max_speed * cell_values)
        split_low = 0.5 * (flux_per_cell - max_speed * cell_values)
        from_left = reconstruct(window(split_high, 0, extent, axis_here), window(split_high, 1, extent, axis_here), window(split_high, 2, extent, axis_here), window(split_high, 3, extent, axis_here), window(split_high, 4, extent, axis_here))
        from_right = reconstruct(window(split_low, 5, extent, axis_here), window(split_low, 4, extent, axis_here), window(split_low, 3, extent, axis_here), window(split_low, 2, extent, axis_here), window(split_low, 1, extent, axis_here))
        face_values = from_left + from_right
        upper_faces = lax.slice_in_dim(face_values, 1, extent + 1, axis=axis_here)
        lower_faces = lax.slice_in_dim(face_values, 0, extent, axis=axis_here)
        results.append(upper_faces - lower_faces)
    return jnp.stack(results)


def advance(padded_field, max_speed):
    interior = padded_field[:, 3:-3, 3:-3, :]
    sweep_first = divergence(padded_field[:, :, 3:-3, :], 1, max_speed)
    sweep_second = divergence(padded_field[:, 3:-3, :, :], 2, max_speed)
    wrapped = jnp.concatenate([interior[:, :, :, -3:], interior, interior[:, :, :, :3]], axis=3)
    sweep_third = divergence(wrapped, 3, max_speed)
    return interior - (courant / max_speed) * (sweep_first + sweep_second + sweep_third)


def silu_derivative(cell_values):
    logistic = jax.nn.sigmoid(cell_values)
    return logistic * (1.0 + cell_values * (1.0 - logistic))


def contract(left, right):
    return lax.dot_general(left, right, (((0,), (0,)), ((), ())), preferred_element_type=jnp.float32)


def train_terms(chosen, targets, dense_first, dense_middle, final_dense_layer, total_rows):
    pre_one = jnp.dot(chosen, dense_first, preferred_element_type=jnp.float32)
    act_one = jax.nn.silu(pre_one).astype(jnp.bfloat16)
    pre_two = jnp.dot(act_one, dense_middle, preferred_element_type=jnp.float32)
    act_two = jax.nn.silu(pre_two).astype(jnp.bfloat16)
    output = lax.dot_general(act_two, final_dense_layer, (((1,), (1,)), ((), ())), preferred_element_type=jnp.float32)
    error_rows = ((output - targets.astype(jnp.float32)) / total_rows).astype(jnp.bfloat16)
    grad_last = contract(error_rows, act_two)
    back_two = jnp.dot(error_rows, final_dense_layer, preferred_element_type=jnp.float32)
    delta_two = (back_two * silu_derivative(pre_two)).astype(jnp.bfloat16)
    grad_middle = contract(act_one, delta_two)
    back_one = lax.dot_general(delta_two, dense_middle, (((1,), (1,)), ((), ())), preferred_element_type=jnp.float32)
    delta_one = (back_one * silu_derivative(pre_one)).astype(jnp.bfloat16)
    grad_first = contract(chosen, delta_one)
    return grad_first, grad_middle, grad_last


def closure(patches, fresh_first, fresh_middle, fresh_last):
    act_one = jax.nn.silu(jnp.dot(patches, fresh_first, preferred_element_type=jnp.float32)).astype(jnp.bfloat16)
    act_two = jax.nn.silu(jnp.dot(act_one, fresh_middle, preferred_element_type=jnp.float32)).astype(jnp.bfloat16)
    return lax.dot_general(act_two, fresh_last, (((1,), (1,)), ((), ())), preferred_element_type=jnp.float32).astype(jnp.bfloat16)


def cut_patches(field):
    blocks = field.reshape(3, N_ROLE, CX // PS, PS, N_BRICK, CY // PS, PS, NZ // PS, PS)
    blocks = blocks.transpose(1, 4, 2, 5, 7, 0, 3, 6, 8)
    return blocks.reshape(N_ROLE * N_BRICK * NP_DEV, F).astype(jnp.bfloat16)


def paste_patches(fix_rows):
    blocks = fix_rows.astype(jnp.float32).reshape(N_ROLE, N_BRICK, CX // PS, CY // PS, NZ // PS, 3, PS, PS, PS)
    blocks = blocks.transpose(5, 0, 2, 6, 1, 3, 7, 4, 8)
    return blocks.reshape(3, NX, NY, NZ)


def reference(velocity, first_layer, middle_layer, last_layer, first_moment, middle_moment, last_moment, patch_pick, target_rows):
    current = velocity
    for number in range(2):
        max_speed = jnp.max(jnp.abs(current))
        padded_field = jnp.pad(current, ((0, 0), (3, 3), (3, 3), (0, 0)), mode="wrap")
        current = advance(padded_field, max_speed)
    patches = cut_patches(velocity)
    row_index = (jnp.arange(NREF, dtype=jnp.int32) // REF_DEV) * NP_DEV + patch_pick.astype(jnp.int32)
    chosen = jnp.take(patches, row_index, axis=0)
    dense_first = first_layer.astype(jnp.bfloat16)
    dense_middle = middle_layer.astype(jnp.bfloat16)
    final_dense_layer = last_layer.astype(jnp.bfloat16)
    grad_first, grad_middle, grad_last = train_terms(chosen, target_rows, dense_first, dense_middle, final_dense_layer, NREF)
    first_momentum = momentum_keep * first_moment + grad_first
    middle_momentum = momentum_keep * middle_moment + grad_middle
    last_momentum = momentum_keep * last_moment + grad_last
    first_updated = first_layer - learn_rate * first_momentum
    middle_updated = middle_layer - learn_rate * middle_momentum
    last_updated = last_layer - learn_rate * last_momentum
    fix_rows = closure(patches, first_updated.astype(jnp.bfloat16), middle_updated.astype(jnp.bfloat16), last_updated.astype(jnp.bfloat16))
    velocity_next = current + paste_patches(fix_rows)
    return (velocity_next, first_updated, middle_updated, last_updated, first_momentum, middle_momentum, last_momentum)
```

```python
import jax
import jax.numpy as jnp
from jax import lax
from jax.experimental import pallas as pl
from jax.experimental.pallas import tpu as pltpu
from jax.sharding import Mesh
from jax.sharding import PartitionSpec as P

PS = 8
AXES = ("role_0", "role_1", "brick_0", "brick_1", "brick_2")
SIZES = (2, 2, 4, 2, 4)
ROLE = ("role_0", "role_1")
BRICK = ("brick_0", "brick_1", "brick_2")
ROWS = (48, 32, 48)
STARTS = (0, 48, 80)
BLOCK = 128
LANES = 256


weno_eps = 1e-06
courant = 0.3
momentum_keep = 0.9
learn_rate = 0.3
bf16 = jnp.bfloat16
f32 = jnp.float32


def flat_id(x, y, z, c):
    return (((x // 2) * 2 + c) * 4 + y) * 8 + (x % 2) * 4 + z


def phase_pairs(phase, shift):
    pairs = []
    for c in range(2):
        dim = (0, 1, 2)[phase] if c == 0 else (2, 0, 1)[phase]
        for x in range(4):
            for y in range(4):
                for z in range(4):
                    to = [x, y, z]
                    to[dim] = (to[dim] + shift) % 4
                    pairs.append((flat_id(x, y, z, c), flat_id(*to, c)))
    return pairs


def order_index(x, y, z, core):
    return z * 16 + y * 4 + x if core == 0 else y * 16 + x * 4 + z


def spread(parts, phase):
    take = (lambda s: parts[s]) if isinstance(parts, (list, tuple)) else (lambda s: parts)
    return [lax.ppermute(take(s), AXES, phase_pairs(phase, s)) for s in (1, 3, 2)]


def swap_cores(array):
    return lax.ppermute(array, "role_1", [(0, 1), (1, 0)])


def places():
    core = lax.axis_index("role_1")
    x = lax.axis_index("role_0") * 2 + lax.axis_index("brick_1")
    y = lax.axis_index("brick_0")
    z = lax.axis_index("brick_2")
    first = jnp.where(core == 0, x, z)
    second = jnp.where(core == 0, y, x)
    third = jnp.where(core == 0, z, y)
    role = lax.axis_index(ROLE)
    return jnp.stack([core, first, second, third, role]).astype(jnp.int32)


VMEM = pl.BlockSpec(memory_space=pltpu.VMEM)
SMEM = pl.BlockSpec(memory_space=pltpu.SMEM)


def call(kernel, outs, place, *arrays, scratch=(), name):
    return pl.pallas_call(
        kernel,
        out_shape=outs,
        in_specs=[SMEM] + [VMEM] * len(arrays),
        out_specs=jax.tree.map(lambda _: VMEM, outs),
        scratch_shapes=scratch,
        name=name,
    )(place, *arrays)


def like(shape, dtype):
    return jax.ShapeDtypeStruct(shape, dtype)


def own_block_kernel(place, first, middle, last, out):
    cols = pl.ds(pl.multiple_of(place[4] * LANES, LANES), LANES)
    for ref, start, rows in zip((first, middle, last), STARTS, ROWS):
        out[start : start + rows, :] = ref[:, cols].astype(bf16)


def put_kernel(which):
    def kernel(place, own, one, three, two, out):
        mine = place[which]
        for s, ref in ((0, own), (1, one), (3, three), (2, two)):
            out[lax.rem(mine + 4 - s, 4)] = ref[...]

    return kernel


def finish_kernel(place, own, one, three, two, first, middle, last):
    core, mine = place[0], place[3]
    for s, ref in ((0, own), (1, one), (3, three), (2, two)):
        at3 = lax.rem(mine + 4 - s, 4)
        for at2 in range(4):
            for at1 in range(4):
                x = jnp.where(core == 0, at1, at2)
                y = jnp.where(core == 0, at2, at3)
                z = jnp.where(core == 0, at3, at1)
                high = x // 2
                brick = y * 8 + (x - high * 2) * 4 + z
                for out, start, rows in zip((first, middle, last), STARTS, ROWS):
                    to = pl.ds(pl.multiple_of(brick * rows, 16), rows)
                    out[high, to, :] = ref[at2, at1, start : start + rows, :]


def gather_matrices(block, place, tag):
    got = spread(block, 0)
    four = call(put_kernel(1), like((4, BLOCK, LANES), bf16), place, block, *got, name=tag + "_put1")
    got = spread(four, 1)
    square = call(
        put_kernel(2), like((4, 4, BLOCK, LANES), bf16), place, four, *got, name=tag + "_put2"
    )
    got = spread(square, 2)
    mine = call(
        finish_kernel,
        tuple(like((2, 32 * rows, LANES), bf16) for rows in ROWS),
        place,
        square,
        *got,
        name=tag + "_put3",
    )
    return mine, tuple(swap_cores(m) for m in mine)


def swap_blocks(tile):
    row = lax.broadcasted_iota(jnp.int32, (16, 128), 0)
    group = lax.broadcasted_iota(jnp.int32, (16, 128), 1) // 8
    for bit in (1, 2, 4, 8):
        row_set = (row & bit) != 0
        group_set = (group & bit) != 0
        down = pltpu.roll(pltpu.roll(tile, 16 - bit, 0), 8 * bit, 1)
        up = pltpu.roll(pltpu.roll(tile, bit, 0), 128 - 8 * bit, 1)
        moved = jnp.where(row_set, up, down)
        tile = jnp.where(row_set == group_set, tile, moved)
    return tile


def cut_kernel(place, field, out):
    for i in range(2):
        for j in range(2):
            for g in range(12):
                c, at = g // 4, i * 8 + (g % 4) * 2
                low = field[c, at, j * 8 : j * 8 + 8, :]
                high = field[c, at + 1, j * 8 : j * 8 + 8, :]
                tile = swap_blocks(jnp.concatenate([low, high], axis=0))
                row = (i * 2 + j) * 16
                out[row : row + 16, g * 128 : g * 128 + 128] = tile.astype(bf16)


def dot(a, b):
    return jnp.dot(a, b, preferred_element_type=f32)


def dot_rows(a, b):
    return lax.dot_general(a, b, (((1,), (1,)), ((), ())), preferred_element_type=f32)


def logistic(v):
    return 1.0 / (1.0 + jnp.exp(-v))


def train_kernel(
    place, patches, pick, targets, m1, m2, m3, o1, o2, o3, keep, send, act, slope_one, slope_two, act_two, delta
):
    core = place[0]
    total = 128 * 128
    cells = [(half, high) for half in range(2) for high in range(2)]
    first, middle, last = (m1, o1), (m2, o2), (m3, o3)

    def role_of(half, high):
        return high * 2 + (core if half == 0 else 1 - core)

    which = lax.broadcasted_iota(jnp.int32, (BLOCK, 64), 1) == pick[...]
    chosen = dot(which.astype(f32).astype(bf16), patches[...]).astype(bf16)
    for half, high in cells:
        pre = dot(chosen, first[half][high])
        s = logistic(pre)
        r = role_of(half, high)
        act[r] = (pre * s).astype(bf16)
        slope_one[r] = s * (1.0 + pre * (1.0 - s))
    act_one = jnp.concatenate([act[r] for r in range(4)], axis=1)
    y = jnp.zeros((BLOCK, 1536), f32)
    for n, (half, high) in enumerate(cells):
        pre = dot(act_one, middle[half][high])
        s = logistic(pre)
        a = (pre * s).astype(bf16)
        act_two[n] = a
        slope_two[n] = s * (1.0 + pre * (1.0 - s))
        y = y + dot_rows(a, last[half][high])
    error = ((y - targets[...].astype(f32)) / total).astype(bf16)

    def store(grad, half, high, m):
        out = keep if half == 0 else send
        target_core = core if half == 0 else 1 - core
        start, rows = STARTS[m], ROWS[m]
        for brick in range(32):
            yy, low, zz = brick // 8, (brick // 4) % 2, brick % 4
            x = high * 2 + low
            at = jnp.where(target_core == 0, order_index(x, yy, zz, 0), order_index(x, yy, zz, 1))
            out[at, start : start + rows, :] = grad[brick * rows : (brick + 1) * rows, :].astype(bf16)

    error_t = error.astype(f32).T.astype(bf16)
    back_one = jnp.zeros((BLOCK, 1024), f32)
    for n, (half, high) in enumerate(cells):
        d = (dot(error, last[half][high]) * slope_two[n]).astype(bf16)
        delta[n] = d
        back_one = back_one + dot_rows(d, middle[half][high])
        store(dot(error_t, act_two[n]), half, high, 2)
    act_t = act_one.astype(f32).T.astype(bf16)
    for n, (half, high) in enumerate(cells):
        store(dot(act_t, delta[n]), half, high, 1)
    for r in range(4):
        act[r] = (back_one[:, r * LANES : (r + 1) * LANES] * slope_one[r]).astype(bf16)
    chosen_t = chosen.astype(f32).T.astype(bf16)
    for half, high in cells:
        store(dot(chosen_t, act[role_of(half, high)]), half, high, 0)


def closure_kernel(place, patches, field, m1, m2, m3, o1, o2, o3, out, act):
    core = place[0]
    cells = [(half, high) for half in range(2) for high in range(2)]
    first, middle, last = (m1, o1), (m2, o2), (m3, o3)
    rows = patches[...]
    for half, high in cells:
        pre = dot(rows, first[half][high])
        act[high * 2 + (core if half == 0 else 1 - core)] = (pre * logistic(pre)).astype(bf16)
    act_one = jnp.concatenate([act[r] for r in range(4)], axis=1)
    fix = jnp.zeros((64, 1536), f32)
    for half, high in cells:
        pre = dot(act_one, middle[half][high])
        fix = fix + dot_rows((pre * logistic(pre)).astype(bf16), last[half][high])
    fix = fix.astype(bf16).astype(f32)
    for i in range(2):
        for j in range(2):
            for g in range(12):
                row = (i * 2 + j) * 16
                tile = swap_blocks(fix[row : row + 16, g * 128 : g * 128 + 128])
                c, at = g // 4, i * 8 + (g % 4) * 2
                for a in range(2):
                    part = tile[a * 8 : a * 8 + 8, :]
                    here = (c, at + a, slice(j * 8, j * 8 + 8))
                    out[here] = field[here] + part


def pair_kernel(place, mine, other, own, one, two, three):
    for s, out in ((1, one), (3, three), (2, two), (0, own)):
        here = pl.ds(lax.rem(place[3] + s, 4) * 16, 16)
        out[...] = (mine[here].astype(f32) + other[here].astype(f32)).astype(bf16)


def total_of(refs, at):
    return sum(ref[at].astype(f32) for ref in refs)


def narrow_kernel(which, width):
    def kernel(place, a, b, c, d, own, one, two, three):
        for s, out in ((1, one), (3, three), (2, two), (0, own)):
            here = pl.ds(lax.rem(place[which] + s, 4) * width, width)
            out[...] = total_of((a, b, c, d), here).astype(bf16)

    return kernel


def update_kernel(place, a, b, c, d, *refs):
    layers, moments, updated, momenta, fresh = refs[:3], refs[3:6], refs[6:9], refs[9:12], refs[12]
    cols = pl.ds(pl.multiple_of(place[4] * LANES, LANES), LANES)
    for m, (start, rows) in enumerate(zip(STARTS, ROWS)):
        here = (0, slice(start, start + rows))
        grad = total_of((a, b, c, d), here)
        momentum = momentum_keep * moments[m][:, cols] + grad
        new = layers[m][:, cols] - learn_rate * momentum
        momenta[m][...] = momentum
        updated[m][...] = new
        fresh[start : start + rows, :] = new.astype(bf16)


def sum_gradients(keep, send, place):
    other = swap_cores(send)
    parts = call(pair_kernel, (like((16, BLOCK, LANES), bf16),) * 4, place, keep, other, name="sum_pair")
    got = spread(parts, 2)
    parts = call(
        narrow_kernel(2, 4), (like((4, BLOCK, LANES), bf16),) * 4, place, parts[0], *got, name="sum_third"
    )
    got = spread(parts, 1)
    parts = call(
        narrow_kernel(1, 1), (like((1, BLOCK, LANES), bf16),) * 4, place, parts[0], *got, name="sum_second"
    )
    got = spread(parts, 0)
    return parts[0], *got


def with_halo(shard, sides, width):
    edges = {}
    for axis, dim in sides:
        size, length = (lax.axis_size(axis), shard.shape[dim])
        up = [(i, (i + 1) % size) for i in range(size)]
        last = lax.slice_in_dim(shard, length - width, length, axis=dim)
        leading = lax.slice_in_dim(shard, 0, width, axis=dim)
        edges[dim] = (
            lax.ppermute(last, axis, up),
            lax.ppermute(leading, axis, [(b, a) for a, b in up]),
        )
    done = []
    for _, dim in sides:
        low, high = edges[dim]
        around = [(width, width) if d in done else (0, 0) for d in range(shard.ndim)]
        shard = jnp.concatenate([jnp.pad(low, around), shard, jnp.pad(high, around)], axis=dim)
        done.append(dim)
    return shard


def reconstruct(cell_one, cell_two, cell_three, cell_four, cell_five):
    guess_low = (2.0 * cell_one - 7.0 * cell_two + 11.0 * cell_three) / 6.0
    guess_center = (-cell_two + 5.0 * cell_three + 2.0 * cell_four) / 6.0
    guess_high = (2.0 * cell_three + 5.0 * cell_four - cell_five) / 6.0
    bend_low = cell_one - 2.0 * cell_two + cell_three
    tilt_low = cell_one - 4.0 * cell_two + 3.0 * cell_three
    bend_center = cell_two - 2.0 * cell_three + cell_four
    tilt_center = cell_two - cell_four
    bend_high = cell_three - 2.0 * cell_four + cell_five
    tilt_high = 3.0 * cell_three - 4.0 * cell_four + cell_five
    rough_low = weno_eps + 13.0 / 12.0 * bend_low * bend_low + 0.25 * tilt_low * tilt_low
    central_smoothness = (
        weno_eps + 13.0 / 12.0 * bend_center * bend_center + 0.25 * tilt_center * tilt_center
    )
    rough_high = weno_eps + 13.0 / 12.0 * bend_high * bend_high + 0.25 * tilt_high * tilt_high
    weight_low = 0.1 / (rough_low * rough_low)
    weight_center = 0.6 / (central_smoothness * central_smoothness)
    weight_high = 0.3 / (rough_high * rough_high)
    blended = weight_low * guess_low + weight_center * guess_center + weight_high * guess_high
    return blended / (weight_low + weight_center + weight_high)


def window(source, offset, extent, axis_here):
    return lax.slice_in_dim(source, offset, offset + extent + 1, axis=axis_here)


def divergence(padded_field, sweep_direction, max_speed):
    axis_here = sweep_direction - 1
    extent = padded_field.shape[sweep_direction] - 6
    carried_state = padded_field[sweep_direction - 1]
    results = []
    for component in range(3):
        cell_values = padded_field[component]
        flux_per_cell = carried_state * cell_values
        split_high = 0.5 * (flux_per_cell + max_speed * cell_values)
        split_low = 0.5 * (flux_per_cell - max_speed * cell_values)
        from_left = reconstruct(
            *(window(split_high, offset, extent, axis_here) for offset in (0, 1, 2, 3, 4))
        )
        from_right = reconstruct(
            *(window(split_low, offset, extent, axis_here) for offset in (5, 4, 3, 2, 1))
        )
        face_values = from_left + from_right
        upper_faces = lax.slice_in_dim(face_values, 1, extent + 1, axis=axis_here)
        lower_faces = lax.slice_in_dim(face_values, 0, extent, axis=axis_here)
        results.append(upper_faces - lower_faces)
    return jnp.stack(results)


def advance(padded_field, max_speed):
    interior = padded_field[:, 3:-3, 3:-3, :]
    sweep_first = divergence(padded_field[:, :, 3:-3, :], 1, max_speed)
    sweep_second = divergence(padded_field[:, 3:-3, :, :], 2, max_speed)
    wrapped = jnp.concatenate([interior[:, :, :, -3:], interior, interior[:, :, :, :3]], axis=3)
    sweep_third = divergence(wrapped, 3, max_speed)
    return interior - courant / max_speed * (sweep_first + sweep_second + sweep_third)


def global_speed(cells):
    own = jnp.broadcast_to(jnp.max(jnp.abs(cells)), (128 * 8, 128))
    return jnp.max(lax.all_to_all(own, AXES, 0, 0, tiled=True))


def one_step(current):
    max_speed = global_speed(current)
    padded = with_halo(current.astype(bf16), ((ROLE, 1), (BRICK, 2)), 3).astype(current.dtype)
    return advance(padded, max_speed)


def shards(velocity, first, middle, last, first_moment, middle_moment, last_moment, patch_pick, targets):
    place = places()
    layers, moments = (first, middle, last), (first_moment, middle_moment, last_moment)
    block = call(own_block_kernel, like((BLOCK, LANES), bf16), place, *layers, name="own_block")
    mine, other = gather_matrices(block, place, "old")
    patches = call(cut_kernel, like((64, 1536), bf16), place, velocity, name="cut")
    between = one_step(velocity)
    keep, send = call(
        train_kernel,
        (like((64, BLOCK, LANES), bf16),) * 2,
        place,
        patches,
        patch_pick.reshape(BLOCK, 1),
        targets,
        *mine,
        *other,
        scratch=[
            pltpu.VMEM((4, BLOCK, LANES), bf16),
            pltpu.VMEM((4, BLOCK, LANES), f32),
            pltpu.VMEM((4, BLOCK, LANES), f32),
            pltpu.VMEM((4, BLOCK, LANES), bf16),
            pltpu.VMEM((4, BLOCK, LANES), bf16),
        ],
        name="train",
    )
    pieces = sum_gradients(keep, send, place)
    wide = tuple(like((rows, LANES), f32) for rows in ROWS)
    results = call(
        update_kernel,
        wide + wide + (like((BLOCK, LANES), bf16),),
        place,
        *pieces,
        *layers,
        *moments,
        name="update",
    )
    mine, other = gather_matrices(results[6], place, "new")
    current = one_step(between)
    velocity_next = call(
        closure_kernel,
        like(velocity.shape, f32),
        place,
        patches,
        current,
        *mine,
        *other,
        scratch=[pltpu.VMEM((4, 64, LANES), bf16)],
        name="closure",
    )
    return (velocity_next, *results[:6])


def solution(mesh):
    torus = Mesh(mesh.devices.reshape(SIZES), AXES)
    in_specs = (P(None, ROLE, BRICK, None),) + (P(BRICK, None),) * 6 + (P(AXES), P(AXES, None))
    out_specs = (P(None, ROLE, BRICK, None),) + (P(BRICK, ROLE),) * 6
    return jax.shard_map(shards, mesh=torus, in_specs=in_specs, out_specs=out_specs, check_vma=False)
```

```python
import math

import jax
import jax.numpy as jnp
from jax import lax
from jax.experimental import pallas as pl
from jax.experimental.pallas import tpu as pltpu
from jax.sharding import Mesh
from jax.sharding import PartitionSpec as P


AXES = ("role_0", "role_1", "brick_0", "brick_1", "brick_2")
SIZES = (2, 2, 4, 2, 4)
ROLE = ("role_0", "role_1")
BRICK = ("brick_0", "brick_1", "brick_2")
ROWS = (48, 32, 48)
STARTS = (0, 48, 80)
BLOCK = 128
LANES = 256


weno_eps = 1e-06
courant = 0.3
momentum_keep = 0.9
learn_rate = 0.3
bf16 = jnp.bfloat16
f32 = jnp.float32


def flat_id(x, y, z, c):
    return (((x // 2) * 2 + c) * 4 + y) * 8 + (x % 2) * 4 + z


def phase_pairs(phase, shift):
    pairs = []
    for c in range(2):
        dim = (0, 1, 2)[phase] if c == 0 else (2, 0, 1)[phase]
        for x in range(4):
            for y in range(4):
                for z in range(4):
                    to = [x, y, z]
                    to[dim] = (to[dim] + shift) % 4
                    pairs.append((flat_id(x, y, z, c), flat_id(*to, c)))
    return pairs


def planes():
    ring = range(4)
    groups = [[flat_id(x, y, z, 0) for y in ring for x in ring] for z in ring]
    return groups + [[flat_id(x, y, z, 1) for x in ring for z in ring] for y in ring]


def exchange_planes(blocks):
    return lax.all_to_all(blocks, AXES, 0, 0, tiled=True, axis_index_groups=planes())


def spread(parts, phase):
    take = (lambda s: parts[s]) if isinstance(parts, (list, tuple)) else (lambda s: parts)
    return [lax.ppermute(take(s), AXES, phase_pairs(phase, s)) for s in (1, 3, 2)]


def swap_cores(array):
    return lax.ppermute(array, "role_1", [(0, 1), (1, 0)])


def places():
    core = lax.axis_index("role_1")
    x = lax.axis_index("role_0") * 2 + lax.axis_index("brick_1")
    y = lax.axis_index("brick_0")
    z = lax.axis_index("brick_2")
    first = jnp.where(core == 0, x, z)
    second = jnp.where(core == 0, y, x)
    third = jnp.where(core == 0, z, y)
    role = lax.axis_index(ROLE)
    return jnp.stack([core, first, second, third, role]).astype(jnp.int32)


VMEM = pl.BlockSpec(memory_space=pltpu.VMEM)
SMEM = pl.BlockSpec(memory_space=pltpu.SMEM)


def held(array):
    return math.prod(array.shape) * jnp.dtype(array.dtype).itemsize


def call(kernel, outs, place, *arrays, scratch=(), spare=4):
    room = sum(map(held, arrays)) + sum(map(held, jax.tree.leaves(outs))) + sum(map(held, scratch))
    return pl.pallas_call(
        kernel,
        out_shape=outs,
        in_specs=[SMEM] + [VMEM] * len(arrays),
        out_specs=jax.tree.map(lambda _: VMEM, outs),
        scratch_shapes=scratch,
        compiler_params=pltpu.CompilerParams(vmem_limit_bytes=room + (spare << 20)),
    )(place, *arrays)


def like(shape, dtype):
    return jax.ShapeDtypeStruct(shape, dtype)


def own_block_kernel(place, first, middle, last, out):
    cols = pl.ds(pl.multiple_of(place[4] * LANES, LANES), LANES)
    for ref, start, rows in zip((first, middle, last), STARTS, ROWS):
        part = ref[:, cols].astype(bf16)
        for copy in range(16):
            out[copy, start : start + rows, :] = part


def finish_kernel(place, own, one, three, two, first, middle, last):
    core, mine = place[0], place[3]
    for s, ref in ((0, own), (1, one), (3, three), (2, two)):
        at3 = lax.rem(mine + 4 - s, 4)
        for at2 in range(4):
            for at1 in range(4):
                x = jnp.where(core == 0, at1, at2)
                y = jnp.where(core == 0, at2, at3)
                z = jnp.where(core == 0, at3, at1)
                high = x // 2
                brick = y * 8 + (x - high * 2) * 4 + z
                for out, start, rows in zip((first, middle, last), STARTS, ROWS):
                    to = pl.ds(pl.multiple_of(brick * rows, 16), rows)
                    out[high, to, :] = ref[at2 * 4 + at1, start : start + rows, :]


def gather_matrices(square, place):
    got = spread(square, 2)
    mine = call(
        finish_kernel,
        tuple(like((2, 32 * rows, LANES), bf16) for rows in ROWS),
        place,
        square,
        *got,
    )
    return mine, tuple(swap_cores(m) for m in mine)


def swap_blocks(tile):
    row = lax.broadcasted_iota(jnp.int32, (16, 128), 0)
    group = lax.broadcasted_iota(jnp.int32, (16, 128), 1) // 8
    for bit in (1, 2, 4, 8):
        row_set = (row & bit) != 0
        group_set = (group & bit) != 0
        down = pltpu.roll(pltpu.roll(tile, 16 - bit, 0), 8 * bit, 1)
        up = pltpu.roll(pltpu.roll(tile, bit, 0), 128 - 8 * bit, 1)
        moved = jnp.where(row_set, up, down)
        tile = jnp.where(row_set == group_set, tile, moved)
    return tile


def cut_kernel(place, field, pick, out, chosen):
    for i in range(2):
        for j in range(2):
            for g in range(12):
                c, at = g // 4, i * 8 + (g % 4) * 2
                low = field[c, at, j * 8 : j * 8 + 8, :]
                high = field[c, at + 1, j * 8 : j * 8 + 8, :]
                tile = swap_blocks(jnp.concatenate([low, high], axis=0))
                row = (i * 2 + j) * 16
                out[row : row + 16, g * 128 : g * 128 + 128] = tile.astype(bf16)
    which = lax.broadcasted_iota(jnp.int32, (BLOCK, 64), 1) == pick[...]
    chosen[...] = dot(which.astype(f32).astype(bf16), out[...]).astype(bf16)


def dot(a, b):
    return jnp.dot(a, b, preferred_element_type=f32)


def dot_rows(a, b):
    return lax.dot_general(a, b, (((1,), (1,)), ((), ())), preferred_element_type=f32)


def logistic(v):
    return 1.0 / (1.0 + jnp.exp(-v))


def forward_kernel(
    place, picked, targets, m1, m2, m3, o1, o2, o3, hold, share, act, slope_one, slope_two, act_two
):
    core = place[0]
    total = 128 * 128
    cells = [(half, high) for half in range(2) for high in range(2)]
    first, middle, last = (m1, o1), (m2, o2), (m3, o3)

    def role_of(half, high):
        return high * 2 + (core if half == 0 else 1 - core)

    chosen = picked[...]
    for half, high in cells:
        pre = dot(chosen, first[half][high])
        s = logistic(pre)
        r = role_of(half, high)
        act[r] = (pre * s).astype(bf16)
        slope_one[r] = s * (1.0 + pre * (1.0 - s))
    act_one = jnp.concatenate([act[r] for r in range(4)], axis=1)
    y = jnp.zeros((BLOCK, 1536), f32)
    for n, (half, high) in enumerate(cells):
        pre = dot(act_one, middle[half][high])
        s = logistic(pre)
        a = (pre * s).astype(bf16)
        act_two[n] = a
        slope_two[n] = s * (1.0 + pre * (1.0 - s))
        y = y + dot_rows(a, last[half][high])
    error = ((y - targets[...].astype(f32)) / total).astype(bf16)
    for out in (hold, share):
        out[:, 0:1536] = error
        out[:, 1536:2560] = act_one
    back_one = jnp.zeros((BLOCK, 1024), f32)
    for n, (half, high) in enumerate(cells):
        d = (dot(error, last[half][high]) * slope_two[n]).astype(bf16)
        out = share if half else hold
        out[:, 2560 + high * LANES : 2816 + high * LANES] = act_two[n]
        out[:, 3072 + high * LANES : 3328 + high * LANES] = d
        back_one = back_one + dot_rows(d, middle[half][high])
    for r in range(4):
        act[r] = (back_one[:, r * LANES : (r + 1) * LANES] * slope_one[r]).astype(bf16)
    for half, high in cells:
        out = share if half else hold
        out[:, 3584 + high * LANES : 3840 + high * LANES] = act[role_of(half, high)]


def gradient_kernel(
    place, hold, other, picked, picked_other, own, one, two, three, left_first, left_middle, left_last
):
    core, mine = place[0], place[3]

    def both(start, size):
        cols = slice(start, start + size)
        return jnp.concatenate([hold[:, cols], other[:, cols]], axis=0)

    def turned(v):
        return v.astype(f32).T.astype(bf16)

    jobs = (
        (2, left_last, both(0, 1536), 2560),
        (1, left_middle, both(1536, 1024), 3072),
        (0, left_first, jnp.concatenate([picked[...], picked_other[...]], axis=0), 3584),
    )
    for m, left, value, start in jobs:
        rows = ROWS[m]
        left[...] = turned(value).reshape(32, rows, LANES)
        for high in range(2):
            right = both(start + high * LANES, LANES)
            for s, out in enumerate((own, one, two, three)):
                at3 = lax.rem(mine + s, 4)
                parts, places_ = [], []
                for low in range(2):
                    for w in range(4):
                        x = high * 2 + low
                        brick = jnp.where(core == 0, w * 8 + at3, at3 * 8 + w) + low * 4
                        parts.append(left[brick])
                        places_.append(jnp.where(core == 0, w * 4 + x, x * 4 + w))
                grad = dot(jnp.concatenate(parts, axis=0), right).astype(bf16)
                for n, at in enumerate(places_):
                    out[at, STARTS[m] : STARTS[m] + rows, :] = grad[n * rows : (n + 1) * rows, :]


def closure_kernel(place, patches, field, m1, m2, m3, o1, o2, o3, out, act):
    core = place[0]
    cells = [(half, high) for half in range(2) for high in range(2)]
    first, middle, last = (m1, o1), (m2, o2), (m3, o3)
    rows = patches[...]
    for half, high in cells:
        pre = dot(rows, first[half][high])
        act[high * 2 + (core if half == 0 else 1 - core)] = (pre * logistic(pre)).astype(bf16)
    act_one = jnp.concatenate([act[r] for r in range(4)], axis=1)
    fix = jnp.zeros((64, 1536), f32)
    for half, high in cells:
        pre = dot(act_one, middle[half][high])
        fix = fix + dot_rows((pre * logistic(pre)).astype(bf16), last[half][high])
    fix = fix.astype(bf16).astype(f32)
    for i in range(2):
        for j in range(2):
            for g in range(12):
                row = (i * 2 + j) * 16
                tile = swap_blocks(fix[row : row + 16, g * 128 : g * 128 + 128])
                c, at = g // 4, i * 8 + (g % 4) * 2
                for a in range(2):
                    part = tile[a * 8 : a * 8 + 8, :]
                    here = (c, at + a, slice(j * 8, j * 8 + 8))
                    out[here] = field[here] + part


def total_of(refs, at):
    return sum(ref[at].astype(f32) for ref in refs)


def third_kernel(place, a, b, c, d, out):
    out[...] = total_of((a, b, c, d), slice(None)).astype(bf16)


def update_kernel(place, pieces, *refs):
    layers, moments, updated, momenta, fresh = refs[:3], refs[3:6], refs[6:9], refs[9:12], refs[12]
    cols = pl.ds(pl.multiple_of(place[4] * LANES, LANES), LANES)
    for m, (start, rows) in enumerate(zip(STARTS, ROWS)):
        grad = sum(pieces[n, start : start + rows, :].astype(f32) for n in range(16))
        momentum = momentum_keep * moments[m][:, cols] + grad
        new = layers[m][:, cols] - learn_rate * momentum
        momenta[m][...] = momentum
        updated[m][...] = new
        for copy in range(16):
            fresh[copy, start : start + rows, :] = new.astype(bf16)


def sum_plane(parts, place):
    got = spread(parts, 2)
    blocks = call(third_kernel, like((16, BLOCK, LANES), bf16), place, parts[0], *got)
    return exchange_planes(blocks)


def with_halo(shard, sides, width):
    edges = {}
    for axis, dim in sides:
        size, length = (lax.axis_size(axis), shard.shape[dim])
        up = [(i, (i + 1) % size) for i in range(size)]
        last = lax.slice_in_dim(shard, length - width, length, axis=dim)
        leading = lax.slice_in_dim(shard, 0, width, axis=dim)
        edges[dim] = (
            lax.ppermute(last, axis, up),
            lax.ppermute(leading, axis, [(b, a) for a, b in up]),
        )
    done = []
    for _, dim in sides:
        low, high = edges[dim]
        around = [(width, width) if d in done else (0, 0) for d in range(shard.ndim)]
        shard = jnp.concatenate([jnp.pad(low, around), shard, jnp.pad(high, around)], axis=dim)
        done.append(dim)
    return shard


def reconstruct(cell_one, cell_two, cell_three, cell_four, cell_five):
    guess_low = (2.0 * cell_one - 7.0 * cell_two + 11.0 * cell_three) / 6.0
    guess_center = (-cell_two + 5.0 * cell_three + 2.0 * cell_four) / 6.0
    guess_high = (2.0 * cell_three + 5.0 * cell_four - cell_five) / 6.0
    bend_low = cell_one - 2.0 * cell_two + cell_three
    tilt_low = cell_one - 4.0 * cell_two + 3.0 * cell_three
    bend_center = cell_two - 2.0 * cell_three + cell_four
    tilt_center = cell_two - cell_four
    bend_high = cell_three - 2.0 * cell_four + cell_five
    tilt_high = 3.0 * cell_three - 4.0 * cell_four + cell_five
    rough_low = weno_eps + 13.0 / 12.0 * bend_low * bend_low + 0.25 * tilt_low * tilt_low
    central_smoothness = (
        weno_eps + 13.0 / 12.0 * bend_center * bend_center + 0.25 * tilt_center * tilt_center
    )
    rough_high = weno_eps + 13.0 / 12.0 * bend_high * bend_high + 0.25 * tilt_high * tilt_high
    weight_low = 0.1 / (rough_low * rough_low)
    weight_center = 0.6 / (central_smoothness * central_smoothness)
    weight_high = 0.3 / (rough_high * rough_high)
    blended = weight_low * guess_low + weight_center * guess_center + weight_high * guess_high
    return blended / (weight_low + weight_center + weight_high)


def window(source, offset, extent, axis_here):
    return lax.slice_in_dim(source, offset, offset + extent + 1, axis=axis_here)


def divergence(padded_field, sweep_direction, max_speed):
    axis_here = sweep_direction - 1
    extent = padded_field.shape[sweep_direction] - 6
    carried_state = padded_field[sweep_direction - 1]
    results = []
    for component in range(3):
        cell_values = padded_field[component]
        flux_per_cell = carried_state * cell_values
        split_high = 0.5 * (flux_per_cell + max_speed * cell_values)
        split_low = 0.5 * (flux_per_cell - max_speed * cell_values)
        from_left = reconstruct(
            *(window(split_high, offset, extent, axis_here) for offset in (0, 1, 2, 3, 4))
        )
        from_right = reconstruct(
            *(window(split_low, offset, extent, axis_here) for offset in (5, 4, 3, 2, 1))
        )
        face_values = from_left + from_right
        upper_faces = lax.slice_in_dim(face_values, 1, extent + 1, axis=axis_here)
        lower_faces = lax.slice_in_dim(face_values, 0, extent, axis=axis_here)
        results.append(upper_faces - lower_faces)
    return jnp.stack(results)


def advance(padded_field, max_speed):
    interior = padded_field[:, 3:-3, 3:-3, :]
    sweep_first = divergence(padded_field[:, :, 3:-3, :], 1, max_speed)
    sweep_second = divergence(padded_field[:, 3:-3, :, :], 2, max_speed)
    wrapped = jnp.concatenate([interior[:, :, :, -3:], interior, interior[:, :, :, :3]], axis=3)
    sweep_third = divergence(wrapped, 3, max_speed)
    return interior - courant / max_speed * (sweep_first + sweep_second + sweep_third)


def global_speed(cells):
    top = jnp.broadcast_to(jnp.max(jnp.abs(cells)), (8, 128))
    top = jnp.maximum(top, swap_cores(top))
    for phase in range(3):
        others = spread(top, phase)
        for other in others:
            top = jnp.maximum(top, other)
    return top[0, 0]


def after(value, first):
    return lax.optimization_barrier((value, first))[0]


def one_step(current, first):
    max_speed = after(global_speed(current), first)
    padded = with_halo(current.astype(bf16), ((ROLE, 1), (BRICK, 2)), 3).astype(current.dtype)
    return advance(padded, max_speed)


def whole(velocity, first, middle, last, first_moment, middle_moment, last_moment, patch_pick, targets):
    place = places()
    layers, moments = (first, middle, last), (first_moment, middle_moment, last_moment)
    copies = call(own_block_kernel, like((16, BLOCK, LANES), bf16), place, *layers)
    square = exchange_planes(copies)
    mine, other = gather_matrices(square, place)
    patches, chosen = call(
        cut_kernel,
        (like((64, 1536), bf16), like((BLOCK, 1536), bf16)),
        place,
        velocity,
        patch_pick.reshape(BLOCK, 1),
    )
    chosen_other = swap_cores(chosen)
    between = one_step(velocity, mine[0])
    hold, share = call(
        forward_kernel,
        (like((BLOCK, 4096), bf16),) * 2,
        place,
        chosen,
        targets,
        *mine,
        *other,
        scratch=[
            pltpu.VMEM((4, BLOCK, LANES), bf16),
            pltpu.VMEM((4, BLOCK, LANES), f32),
            pltpu.VMEM((4, BLOCK, LANES), f32),
            pltpu.VMEM((4, BLOCK, LANES), bf16),
        ],
    )
    parts = call(
        gradient_kernel,
        (like((16, BLOCK, LANES), bf16),) * 4,
        place,
        hold,
        swap_cores(share),
        chosen,
        chosen_other,
        scratch=[pltpu.VMEM((32, rows, LANES), bf16) for rows in ROWS],
    )
    between = after(between, parts[3])
    pieces = sum_plane(parts, place)
    wide = tuple(like((rows, LANES), f32) for rows in ROWS)
    results = call(
        update_kernel,
        wide + wide + (like((16, BLOCK, LANES), bf16),),
        place,
        pieces,
        *layers,
        *moments,
    )
    mine, other = gather_matrices(exchange_planes(results[6]), place)
    current = one_step(between, results[6])
    velocity_next = call(
        closure_kernel,
        like(velocity.shape, f32),
        place,
        patches,
        current,
        *mine,
        *other,
        scratch=[pltpu.VMEM((4, 64, LANES), bf16)],
    )
    return (velocity_next, *results[:6])


def solution(mesh):
    torus = Mesh(mesh.devices.reshape(SIZES), AXES)
    in_specs = (P(None, ROLE, BRICK, None),) + (P(BRICK, None),) * 6 + (P(AXES), P(AXES, None))
    out_specs = (P(None, ROLE, BRICK, None),) + (P(BRICK, ROLE),) * 6
    return jax.shard_map(whole, mesh=torus, in_specs=in_specs, out_specs=out_specs, check_vma=False)
```

```python
import math

import jax
import jax.numpy as jnp
from jax import lax
from jax.experimental import pallas as pl
from jax.experimental.pallas import tpu as pltpu
from jax.sharding import Mesh
from jax.sharding import PartitionSpec as P


AXES = ("role_0", "role_1", "brick_0", "brick_1", "brick_2")
SIZES = (2, 2, 4, 2, 4)
ROLE = ("role_0", "role_1")
BRICK = ("brick_0", "brick_1", "brick_2")
ROWS = (48, 32, 48)
STARTS = (0, 48, 80)
BLOCK = 128
LANES = 256


weno_eps = 1e-06
courant = 0.3
momentum_keep = 0.9
learn_rate = 0.3
bf16 = jnp.bfloat16
f32 = jnp.float32


def flat_id(x, y, z, c):
    return (((x // 2) * 2 + c) * 4 + y) * 8 + (x % 2) * 4 + z


def phase_pairs(phase, shift):
    pairs = []
    for c in range(2):
        dim = (0, 1, 2)[phase] if c == 0 else (2, 0, 1)[phase]
        for x in range(4):
            for y in range(4):
                for z in range(4):
                    to = [x, y, z]
                    to[dim] = (to[dim] + shift) % 4
                    pairs.append((flat_id(x, y, z, c), flat_id(*to, c)))
    return pairs


def planes():
    ring = range(4)
    groups = [[flat_id(x, y, z, 0) for y in ring for x in ring] for z in ring]
    return groups + [[flat_id(x, y, z, 1) for x in ring for z in ring] for y in ring]


def exchange_planes(blocks):
    return lax.all_to_all(blocks, AXES, 0, 0, tiled=True, axis_index_groups=planes())


def spread(parts, phase):
    take = (lambda s: parts[s]) if isinstance(parts, (list, tuple)) else (lambda s: parts)
    return [lax.ppermute(take(s), AXES, phase_pairs(phase, s)) for s in (1, 3, 2)]


def swap_cores(array):
    return lax.ppermute(array, "role_1", [(0, 1), (1, 0)])


def places():
    core = lax.axis_index("role_1")
    x = lax.axis_index("role_0") * 2 + lax.axis_index("brick_1")
    y = lax.axis_index("brick_0")
    z = lax.axis_index("brick_2")
    first = jnp.where(core == 0, x, z)
    second = jnp.where(core == 0, y, x)
    third = jnp.where(core == 0, z, y)
    role = lax.axis_index(ROLE)
    return jnp.stack([core, first, second, third, role]).astype(jnp.int32)


VMEM = pl.BlockSpec(memory_space=pltpu.VMEM)
SMEM = pl.BlockSpec(memory_space=pltpu.SMEM)


def held(array):
    return math.prod(array.shape) * jnp.dtype(array.dtype).itemsize


def call(kernel, outs, place, *arrays, scratch=(), spare=4):
    room = sum(map(held, arrays)) + sum(map(held, jax.tree.leaves(outs))) + sum(map(held, scratch))
    return pl.pallas_call(
        kernel,
        out_shape=outs,
        in_specs=[SMEM] + [VMEM] * len(arrays),
        out_specs=jax.tree.map(lambda _: VMEM, outs),
        scratch_shapes=scratch,
        compiler_params=pltpu.CompilerParams(vmem_limit_bytes=room + (spare << 20)),
    )(place, *arrays)


def like(shape, dtype):
    return jax.ShapeDtypeStruct(shape, dtype)


def own_block_kernel(place, first, middle, last, out):
    cols = pl.ds(pl.multiple_of(place[4] * LANES, LANES), LANES)
    for ref, start, rows in zip((first, middle, last), STARTS, ROWS):
        part = ref[:, cols].astype(bf16)
        for copy in range(16):
            out[copy, start : start + rows, :] = part


def finish_kernel(place, own, one, three, two, first, middle, last):
    core, mine = place[0], place[3]
    for s, ref in ((0, own), (1, one), (3, three), (2, two)):
        at3 = lax.rem(mine + 4 - s, 4)
        for at2 in range(4):
            for at1 in range(4):
                x = jnp.where(core == 0, at1, at2)
                y = jnp.where(core == 0, at2, at3)
                z = jnp.where(core == 0, at3, at1)
                high = x // 2
                brick = y * 8 + (x - high * 2) * 4 + z
                for out, start, rows in zip((first, middle, last), STARTS, ROWS):
                    to = pl.ds(pl.multiple_of(brick * rows, 16), rows)
                    out[high, to, :] = ref[at2 * 4 + at1, start : start + rows, :]


def gather_matrices(square, place):
    got = spread(square, 2)
    mine = call(finish_kernel, tuple(like((2, 32 * rows, LANES), bf16) for rows in ROWS), place, square, *got)
    return mine, tuple(swap_cores(m) for m in mine)


def swap_blocks(tile):
    row = lax.broadcasted_iota(jnp.int32, (16, 128), 0)
    group = lax.broadcasted_iota(jnp.int32, (16, 128), 1) // 8
    for bit in (1, 2, 4, 8):
        row_set = (row & bit) != 0
        group_set = (group & bit) != 0
        down = pltpu.roll(pltpu.roll(tile, 16 - bit, 0), 8 * bit, 1)
        up = pltpu.roll(pltpu.roll(tile, bit, 0), 128 - 8 * bit, 1)
        moved = jnp.where(row_set, up, down)
        tile = jnp.where(row_set == group_set, tile, moved)
    return tile


def cut_kernel(place, field, pick, out, chosen):
    for i in range(2):
        for j in range(2):
            for g in range(12):
                c, at = g // 4, i * 8 + (g % 4) * 2
                low = field[c, at, j * 8 : j * 8 + 8, :]
                high = field[c, at + 1, j * 8 : j * 8 + 8, :]
                tile = swap_blocks(jnp.concatenate([low, high], axis=0))
                row = (i * 2 + j) * 16
                out[row : row + 16, g * 128 : g * 128 + 128] = tile.astype(bf16)
    which = lax.broadcasted_iota(jnp.int32, (BLOCK, 64), 1) == pick[...]
    chosen[...] = dot(which.astype(f32).astype(bf16), out[...]).astype(bf16)


def top_kernel(place, field, out):
    def take(n, top):
        return jnp.maximum(top, jnp.max(jnp.abs(field[n // 16, n % 16]).reshape(2, 8, 128), axis=0))

    out[...] = lax.fori_loop(0, 48, take, jnp.zeros((8, 128), f32))


def dot(a, b):
    return jnp.dot(a, b, preferred_element_type=f32)


def dot_rows(a, b):
    return lax.dot_general(a, b, (((1,), (1,)), ((), ())), preferred_element_type=f32)


def logistic(v):
    return 1.0 / (1.0 + jnp.exp(-v))


def forward_kernel(
    place, picked, targets, m1, m2, m3, o1, o2, o3, hold, share, act, slope_one, slope_two, act_two
):
    core = place[0]
    total = 128 * 128
    cells = [(half, high) for half in range(2) for high in range(2)]
    first, middle, last = (m1, o1), (m2, o2), (m3, o3)

    def role_of(half, high):
        return high * 2 + (core if half == 0 else 1 - core)

    chosen = picked[...]
    for half, high in cells:
        pre = dot(chosen, first[half][high])
        s = logistic(pre)
        r = role_of(half, high)
        act[r] = (pre * s).astype(bf16)
        slope_one[r] = s * (1.0 + pre * (1.0 - s))
    act_one = jnp.concatenate([act[r] for r in range(4)], axis=1)
    y = jnp.zeros((BLOCK, 1536), f32)
    for n, (half, high) in enumerate(cells):
        pre = dot(act_one, middle[half][high])
        s = logistic(pre)
        a = (pre * s).astype(bf16)
        act_two[n] = a
        slope_two[n] = s * (1.0 + pre * (1.0 - s))
        y = y + dot_rows(a, last[half][high])
    error = ((y - targets[...].astype(f32)) / total).astype(bf16)
    for out in (hold, share):
        out[:, 0:1536] = error
        out[:, 1536:2560] = act_one
    back_one = jnp.zeros((BLOCK, 1024), f32)
    for n, (half, high) in enumerate(cells):
        d = (dot(error, last[half][high]) * slope_two[n]).astype(bf16)
        out = share if half else hold
        out[:, 2560 + high * LANES : 2816 + high * LANES] = act_two[n]
        out[:, 3072 + high * LANES : 3328 + high * LANES] = d
        back_one = back_one + dot_rows(d, middle[half][high])
    for r in range(4):
        act[r] = (back_one[:, r * LANES : (r + 1) * LANES] * slope_one[r]).astype(bf16)
    for half, high in cells:
        out = share if half else hold
        out[:, 3584 + high * LANES : 3840 + high * LANES] = act[role_of(half, high)]


def gradient_kernel(
    place, hold, other, picked, picked_other, own, one, two, three, left_first, left_middle, left_last
):
    core, mine = place[0], place[3]

    def both(start, size):
        cols = slice(start, start + size)
        return jnp.concatenate([hold[:, cols], other[:, cols]], axis=0)

    def turned(v):
        return v.astype(f32).T.astype(bf16)

    jobs = (
        (2, left_last, both(0, 1536), 2560),
        (1, left_middle, both(1536, 1024), 3072),
        (0, left_first, jnp.concatenate([picked[...], picked_other[...]], axis=0), 3584),
    )
    for m, left, value, start in jobs:
        rows = ROWS[m]
        left[...] = turned(value).reshape(32, rows, LANES)
        for high in range(2):
            right = both(start + high * LANES, LANES)
            for s, out in enumerate((own, one, two, three)):
                at3 = lax.rem(mine + s, 4)
                parts, places_ = [], []
                for low in range(2):
                    for w in range(4):
                        x = high * 2 + low
                        brick = jnp.where(core == 0, w * 8 + at3, at3 * 8 + w) + low * 4
                        parts.append(left[brick])
                        places_.append(jnp.where(core == 0, w * 4 + x, x * 4 + w))
                grad = dot(jnp.concatenate(parts, axis=0), right).astype(bf16)
                for n, at in enumerate(places_):
                    out[at, STARTS[m] : STARTS[m] + rows, :] = grad[n * rows : (n + 1) * rows, :]


def closure_kernel(place, patches, field, m1, m2, m3, o1, o2, o3, out, act):
    core = place[0]
    cells = [(half, high) for half in range(2) for high in range(2)]
    first, middle, last = (m1, o1), (m2, o2), (m3, o3)
    rows = patches[...]
    for half, high in cells:
        pre = dot(rows, first[half][high])
        act[high * 2 + (core if half == 0 else 1 - core)] = (pre * logistic(pre)).astype(bf16)
    act_one = jnp.concatenate([act[r] for r in range(4)], axis=1)
    fix = jnp.zeros((64, 1536), f32)
    for half, high in cells:
        pre = dot(act_one, middle[half][high])
        fix = fix + dot_rows((pre * logistic(pre)).astype(bf16), last[half][high])
    fix = fix.astype(bf16).astype(f32)
    for i in range(2):
        for j in range(2):
            for g in range(12):
                row = (i * 2 + j) * 16
                tile = swap_blocks(fix[row : row + 16, g * 128 : g * 128 + 128])
                c, at = g // 4, i * 8 + (g % 4) * 2
                for a in range(2):
                    part = tile[a * 8 : a * 8 + 8, :]
                    here = (c, at + a, slice(j * 8, j * 8 + 8))
                    out[here] = field[here] + part


def total_of(refs, at):
    return sum(ref[at].astype(f32) for ref in refs)


def third_kernel(place, a, b, c, d, out):
    out[...] = total_of((a, b, c, d), slice(None)).astype(bf16)


def update_kernel(place, pieces, *refs):
    layers, moments, updated, momenta, fresh = refs[:3], refs[3:6], refs[6:9], refs[9:12], refs[12]
    cols = pl.ds(pl.multiple_of(place[4] * LANES, LANES), LANES)
    for m, (start, rows) in enumerate(zip(STARTS, ROWS)):
        grad = sum(pieces[n, start : start + rows, :].astype(f32) for n in range(16))
        momentum = momentum_keep * moments[m][:, cols] + grad
        new = layers[m][:, cols] - learn_rate * momentum
        momenta[m][...] = momentum
        updated[m][...] = new
        for copy in range(16):
            fresh[copy, start : start + rows, :] = new.astype(bf16)


def sum_plane(parts, place):
    got = spread(parts, 2)
    blocks = call(third_kernel, like((16, BLOCK, LANES), bf16), place, parts[0], *got)
    return exchange_planes(blocks)


def edges_of(field):
    rounded, found = field.astype(bf16), []
    for axis, dim in ((ROLE, 1), (BRICK, 2)):
        size, length = lax.axis_size(axis), field.shape[dim]
        up = [(i, (i + 1) % size) for i in range(size)]
        last = lax.slice_in_dim(rounded, length - 3, length, axis=dim)
        leading = lax.slice_in_dim(rounded, 0, 3, axis=dim)
        found.append(lax.ppermute(last, axis, up).astype(f32))
        found.append(lax.ppermute(leading, axis, [(b, a) for a, b in up]).astype(f32))
    return found


def blended(a, b, c, d, e):
    bend, tilt, floor = 13.0 / 12.0 / 64.0, 0.25 / 64.0, weno_eps / 64.0
    b0, b1, b2 = a - 2.0 * b + c, b - 2.0 * c + d, c - 2.0 * d + e
    t0, t1, t2 = a - 4.0 * b + 3.0 * c, b - d, 3.0 * c - 4.0 * d + e
    r0 = floor + bend * b0 * b0 + tilt * t0 * t0
    r1 = floor + bend * b1 * b1 + tilt * t1 * t1
    r2 = floor + bend * b2 * b2 + tilt * t2 * t2
    s0, s1, s2 = r0 * r0, r1 * r1, r2 * r2
    w0, w1, w2 = 0.1 * (s1 * s2), 0.6 * (s0 * s2), 0.3 * (s0 * s1)
    upper = w0 * (2.0 * a - 7.0 * b + 11.0 * c) + w1 * (5.0 * c + 2.0 * d - b) + w2 * (2.0 * c + 5.0 * d - e)
    return upper / (6.0 * (w0 + w1 + w2))


def face(plus, minus):
    return blended(*plus[0:5]) + blended(*minus[5:0:-1])


def advect_kernel(tops, field, low_x, high_x, low_y, high_y, out, top, plus_x, minus_x, rows, plus_y, minus_y, faces):
    speed = jnp.max(tops[...])

    def split(along, value):
        return 0.5 * (along * value + speed * value), 0.5 * (along * value - speed * value)

    def lay(at, planes):
        for c in range(3):
            plus_x[c, at], minus_x[c, at] = split(planes[0], planes[c])

    for n in range(3):
        lay(n, [low_x[c, n] for c in range(3)])
        lay(n + 19, [high_x[c, n] for c in range(3)])

    def inner(n, carry):
        lay(n + 3, [field[c, n] for c in range(3)])
        return carry

    lax.fori_loop(0, 16, inner, 0)
    factor = courant / speed
    top[...] = jnp.zeros((8, 128), f32)

    def face_x(c, n):
        return face([plus_x[c, n + k] for k in range(6)], [minus_x[c, n + k] for k in range(6)])

    def step(n, below):
        above = tuple(face_x(c, n + 1) for c in range(3))
        values = [field[c, n] for c in range(3)]
        for c in range(3):
            rows[c, 0:3, :] = low_y[c, n]
            rows[c, 3:19, :] = values[c]
            rows[c, 19:22, :] = high_y[c, n]
        for c in range(3):
            plus_y[...], minus_y[...] = split(rows[1], rows[c])
            faces[...] = face(
                [plus_y[k : k + 24, :] for k in range(6)], [minus_y[k : k + 24, :] for k in range(6)]
            )
            along_y = faces[1:17, :] - faces[0:16, :]
            plus, minus = split(values[2], values[c])
            shifts = (2, 1, 0, 127, 126, 125)
            edge = face(
                [pltpu.roll(plus, k, 1) if k else plus for k in shifts],
                [pltpu.roll(minus, k, 1) if k else minus for k in shifts],
            )
            along_z = edge - pltpu.roll(edge, 1, 1)
            new = values[c] - factor * ((above[c] - below[c]) + along_y + along_z)
            out[c, n] = new
            size = jnp.abs(new)
            top[...] = jnp.maximum(top[...], jnp.maximum(size[0:8, :], size[8:16, :]))
        return above

    lax.fori_loop(0, 16, step, tuple(face_x(c, 0) for c in range(3)))


def advect(tops, field, edges):
    planes, line = (3, 22, 16, 128), (32, 128)
    scratch = [pltpu.VMEM(planes, f32)] * 2 + [pltpu.VMEM((3, *line), f32)]
    scratch += [pltpu.VMEM(line, f32)] * 2 + [pltpu.VMEM((24, 128), f32)]
    return pl.pallas_call(
        advect_kernel,
        out_shape=(like(field.shape, f32), like((8, 128), f32)),
        in_specs=[VMEM] * 6,
        out_specs=(VMEM, VMEM),
        scratch_shapes=scratch,
        compiler_params=pltpu.CompilerParams(vmem_limit_bytes=8 << 20),
    )(tops, field, *edges)


def global_tops(top):
    other = swap_cores(top)
    top = jnp.maximum(top, other)
    for phase in range(3):
        others = spread(top, phase)
        for other in others:
            top = jnp.maximum(top, other)
    return top


def after(value, first):
    return lax.optimization_barrier((value, first))[0]


def one_step(current, top, first):
    tops = after(global_tops(top), first)
    edges = edges_of(current)
    return advect(tops, current, edges)


def whole(velocity, first, middle, last, first_moment, middle_moment, last_moment, patch_pick, targets):
    place = places()
    layers, moments = (first, middle, last), (first_moment, middle_moment, last_moment)
    copies = call(own_block_kernel, like((16, BLOCK, LANES), bf16), place, *layers)
    square = exchange_planes(copies)
    mine, other = gather_matrices(square, place)
    top = call(top_kernel, like((8, 128), f32), place, velocity)
    patches, chosen = call(
        cut_kernel, (like((64, 1536), bf16), like((BLOCK, 1536), bf16)), place, velocity, patch_pick.reshape(BLOCK, 1)
    )
    chosen_other = swap_cores(chosen)
    between, top = one_step(velocity, top, mine[0])
    hold, share = call(
        forward_kernel,
        (like((BLOCK, 4096), bf16),) * 2,
        place,
        chosen,
        targets,
        *mine,
        *other,
        scratch=[
            pltpu.VMEM((4, BLOCK, LANES), bf16),
            pltpu.VMEM((4, BLOCK, LANES), f32),
            pltpu.VMEM((4, BLOCK, LANES), f32),
            pltpu.VMEM((4, BLOCK, LANES), bf16),
        ],
    )
    parts = call(
        gradient_kernel,
        (like((16, BLOCK, LANES), bf16),) * 4,
        place,
        hold,
        swap_cores(share),
        chosen,
        chosen_other,
        scratch=[pltpu.VMEM((32, rows, LANES), bf16) for rows in ROWS],
    )
    between, top = lax.optimization_barrier((between, top, parts[3]))[:2]
    pieces = sum_plane(parts, place)
    wide = tuple(like((rows, LANES), f32) for rows in ROWS)
    results = call(update_kernel, wide + wide + (like((16, BLOCK, LANES), bf16),), place, pieces, *layers, *moments)
    mine, other = gather_matrices(exchange_planes(results[6]), place)
    current, _ = one_step(between, top, results[6])
    velocity_next = call(
        closure_kernel,
        like(velocity.shape, f32),
        place,
        patches,
        current,
        *mine,
        *other,
        scratch=[pltpu.VMEM((4, 64, LANES), bf16)],
    )
    return (velocity_next, *results[:6])


def solution(mesh):
    torus = Mesh(mesh.devices.reshape(SIZES), AXES)
    in_specs = (P(None, ROLE, BRICK, None),) + (P(BRICK, None),) * 6 + (P(AXES), P(AXES, None))
    out_specs = (P(None, ROLE, BRICK, None),) + (P(BRICK, ROLE),) * 6
    return jax.shard_map(whole, mesh=torus, in_specs=in_specs, out_specs=out_specs, check_vma=False)
```

```python
import math

import jax
import jax.numpy as jnp
from jax import lax
from jax.experimental import pallas as pl
from jax.experimental.pallas import tpu as pltpu
from jax.sharding import Mesh
from jax.sharding import PartitionSpec as P


AXES = ("role_0", "role_1", "brick_0", "brick_1", "brick_2")
SIZES = (2, 2, 4, 2, 4)
ROLE = ("role_0", "role_1")
BRICK = ("brick_0", "brick_1", "brick_2")
ROWS = (48, 32, 48)
STARTS = (0, 48, 80)
BLOCK = 128
LANES = 256


weno_eps = 1e-06
courant = 0.3
momentum_keep = 0.9
learn_rate = 0.3
bf16 = jnp.bfloat16
f32 = jnp.float32


def flat_id(x, y, z, c):
    return (((x // 2) * 2 + c) * 4 + y) * 8 + (x % 2) * 4 + z


def phase_pairs(phase, shift):
    pairs = []
    for c in range(2):
        dim = (0, 1, 2)[phase] if c == 0 else (2, 0, 1)[phase]
        for x in range(4):
            for y in range(4):
                for z in range(4):
                    to = [x, y, z]
                    to[dim] = (to[dim] + shift) % 4
                    pairs.append((flat_id(x, y, z, c), flat_id(*to, c)))
    return pairs


def planes():
    ring = range(4)
    groups = [[flat_id(x, y, z, 0) for y in ring for x in ring] for z in ring]
    return groups + [[flat_id(x, y, z, 1) for x in ring for z in ring] for y in ring]


def exchange_planes(blocks):
    return lax.all_to_all(blocks, AXES, 0, 0, tiled=True, axis_index_groups=planes())


def spread(parts, phase):
    take = (lambda s: parts[s]) if isinstance(parts, (list, tuple)) else (lambda s: parts)
    return [lax.ppermute(take(s), AXES, phase_pairs(phase, s)) for s in (1, 3, 2)]


def swap_cores(array):
    return lax.ppermute(array, "role_1", [(0, 1), (1, 0)])


def places():
    core = lax.axis_index("role_1")
    x = lax.axis_index("role_0") * 2 + lax.axis_index("brick_1")
    y = lax.axis_index("brick_0")
    z = lax.axis_index("brick_2")
    first = jnp.where(core == 0, x, z)
    second = jnp.where(core == 0, y, x)
    third = jnp.where(core == 0, z, y)
    role = lax.axis_index(ROLE)
    beside = jnp.where(core == 0, y, z)
    return jnp.stack([core, first, second, third, role, beside]).astype(jnp.int32)


VMEM = pl.BlockSpec(memory_space=pltpu.VMEM)
SMEM = pl.BlockSpec(memory_space=pltpu.SMEM)


def held(array):
    return math.prod(array.shape) * jnp.dtype(array.dtype).itemsize


def call(kernel, outs, place, *arrays, scratch=(), spare=4):
    room = sum(map(held, arrays)) + sum(map(held, jax.tree.leaves(outs))) + sum(map(held, scratch))
    return pl.pallas_call(
        kernel,
        out_shape=outs,
        in_specs=[SMEM] + [VMEM] * len(arrays),
        out_specs=jax.tree.map(lambda _: VMEM, outs),
        scratch_shapes=scratch,
        compiler_params=pltpu.CompilerParams(vmem_limit_bytes=room + (spare << 20)),
    )(place, *arrays)


def like(shape, dtype):
    return jax.ShapeDtypeStruct(shape, dtype)


def own_block_kernel(place, first, middle, last, out):
    for ref, start, rows in zip((first, middle, last), STARTS, ROWS):
        part = ref[...].astype(bf16)
        for copy in range(16):
            out[copy, start : start + rows, :] = part


def own_block(place, layers):
    grid = pltpu.PrefetchScalarGridSpec(
        num_scalar_prefetch=1,
        grid=(1,),
        in_specs=[pl.BlockSpec((rows, LANES), lambda i, place: (0, place[4])) for rows in ROWS],
        out_specs=pl.BlockSpec((16, BLOCK, LANES), lambda i, place: (0, 0, 0)),
    )
    return pl.pallas_call(
        own_block_kernel,
        out_shape=like((16, BLOCK, LANES), bf16),
        grid_spec=grid,
        compiler_params=pltpu.CompilerParams(vmem_limit_bytes=8 << 20),
        name="own_block",
    )(place, *layers)


def finish_kernel(of_other):
    def kernel(place, own, one, three, low, high_part, first, middle, last):
        core = 1 - place[0] if of_other else place[0]
        mine = place[5] if of_other else place[3]
        for s, ref in ((0, own), (1, one), (3, three), (2, None)):
            at3 = lax.rem(mine + 4 - s, 4)
            for at2 in range(4):
                for at1 in range(4):
                    n = at2 * 4 + at1
                    source, at = (ref, n) if ref is not None else ((low, n) if n < 8 else (high_part, n - 8))
                    x = jnp.where(core == 0, at1, at2)
                    y = jnp.where(core == 0, at2, at3)
                    z = jnp.where(core == 0, at3, at1)
                    high = x // 2
                    brick = y * 8 + (x - high * 2) * 4 + z
                    for out, start, rows in zip((first, middle, last), STARTS, ROWS):
                        to = pl.ds(pl.multiple_of(brick * rows, 16), rows)
                        out[high, to, :] = source[at, start : start + rows, :]

    return kernel


def gather_matrices(square, place):
    def shifted(array, shift):
        return lax.ppermute(array, AXES, phase_pairs(2, shift))

    def finish(pieces, of_other):
        return call(
            finish_kernel(of_other),
            tuple(like((2, 32 * rows, LANES), bf16) for rows in ROWS),
            place,
            *pieces,
        )

    one, three = shifted(square, 1), shifted(square, 3)
    given = [swap_cores(square)]
    low, high = shifted(one[:8], 1), shifted(three[8:], 3)
    given += [swap_cores(one), swap_cores(three)]
    given += [swap_cores(low), swap_cores(high)]
    mine = finish((square, one, three, low, high), False)
    return mine, finish(given, True)


def swap_blocks(tile):
    row = lax.broadcasted_iota(jnp.int32, (16, 128), 0)
    group = lax.broadcasted_iota(jnp.int32, (16, 128), 1) // 8
    for bit in (1, 2, 4, 8):
        row_set = (row & bit) != 0
        group_set = (group & bit) != 0
        down = pltpu.roll(pltpu.roll(tile, 16 - bit, 0), 8 * bit, 1)
        up = pltpu.roll(pltpu.roll(tile, bit, 0), 128 - 8 * bit, 1)
        moved = jnp.where(row_set, up, down)
        tile = jnp.where(row_set == group_set, tile, moved)
    return tile


def cut_kernel(place, field, pick, out, chosen):
    for i in range(2):
        for j in range(2):
            for g in range(12):
                c, at = g // 4, i * 8 + (g % 4) * 2
                low = field[c, at, j * 8 : j * 8 + 8, :]
                high = field[c, at + 1, j * 8 : j * 8 + 8, :]
                tile = swap_blocks(jnp.concatenate([low, high], axis=0))
                row = (i * 2 + j) * 16
                out[row : row + 16, g * 128 : g * 128 + 128] = tile.astype(bf16)
    which = lax.broadcasted_iota(jnp.int32, (BLOCK, 64), 1) == pick[...]
    chosen[...] = dot(which.astype(f32).astype(bf16), out[...]).astype(bf16)


def top_kernel(place, field, out):
    def take(n, top):
        return jnp.maximum(top, jnp.max(jnp.abs(field[n // 16, n % 16]).reshape(2, 8, 128), axis=0))

    out[...] = lax.fori_loop(0, 48, take, jnp.zeros((8, 128), f32))


def dot(a, b):
    return jnp.dot(a, b, preferred_element_type=f32)


def dot_rows(a, b):
    return lax.dot_general(a, b, (((1,), (1,)), ((), ())), preferred_element_type=f32)


def logistic(v):
    return 1.0 / (1.0 + jnp.exp(-v))


def forward_kernel(
    place, picked, targets, m1, m2, m3, o1, o2, o3, hold, share, act, slope_one, slope_two, act_two
):
    core = place[0]
    total = 128 * 128
    cells = [(half, high) for half in range(2) for high in range(2)]
    first, middle, last = (m1, o1), (m2, o2), (m3, o3)

    def role_of(half, high):
        return high * 2 + (core if half == 0 else 1 - core)

    chosen = picked[...]
    for half, high in cells:
        pre = dot(chosen, first[half][high])
        s = logistic(pre)
        r = role_of(half, high)
        act[r] = (pre * s).astype(bf16)
        slope_one[r] = s * (1.0 + pre * (1.0 - s))
    act_one = jnp.concatenate([act[r] for r in range(4)], axis=1)
    y = jnp.zeros((BLOCK, 1536), f32)
    for n, (half, high) in enumerate(cells):
        pre = dot(act_one, middle[half][high])
        s = logistic(pre)
        a = (pre * s).astype(bf16)
        act_two[n] = a
        slope_two[n] = s * (1.0 + pre * (1.0 - s))
        y = y + dot_rows(a, last[half][high])
    error = ((y - targets[...].astype(f32)) / total).astype(bf16)
    for out in (hold, share):
        out[:, 0:1536] = error
        out[:, 1536:2560] = act_one
    back_one = jnp.zeros((BLOCK, 1024), f32)
    for n, (half, high) in enumerate(cells):
        d = (dot(error, last[half][high]) * slope_two[n]).astype(bf16)
        out = share if half else hold
        out[:, 2560 + high * LANES : 2816 + high * LANES] = act_two[n]
        out[:, 3072 + high * LANES : 3328 + high * LANES] = d
        back_one = back_one + dot_rows(d, middle[half][high])
    for r in range(4):
        act[r] = (back_one[:, r * LANES : (r + 1) * LANES] * slope_one[r]).astype(bf16)
    for half, high in cells:
        out = share if half else hold
        out[:, 3584 + high * LANES : 3840 + high * LANES] = act[role_of(half, high)]


def gradient_kernel(
    place, hold, other, picked, picked_other, own, one, two, three, left_first, left_middle, left_last
):
    core, mine = place[0], place[3]

    def both(start, size):
        cols = slice(start, start + size)
        return jnp.concatenate([hold[:, cols], other[:, cols]], axis=0)

    def turned(v):
        return v.astype(f32).T.astype(bf16)

    jobs = (
        (2, left_last, both(0, 1536), 2560),
        (1, left_middle, both(1536, 1024), 3072),
        (0, left_first, jnp.concatenate([picked[...], picked_other[...]], axis=0), 3584),
    )
    for m, left, value, start in jobs:
        rows = ROWS[m]
        left[...] = turned(value).reshape(32, rows, LANES)
        for high in range(2):
            right = both(start + high * LANES, LANES)
            for s, out in enumerate((own, one, two, three)):
                at3 = lax.rem(mine + s, 4)
                parts, places_ = [], []
                for low in range(2):
                    for w in range(4):
                        x = high * 2 + low
                        brick = jnp.where(core == 0, w * 8 + at3, at3 * 8 + w) + low * 4
                        parts.append(left[brick])
                        places_.append(jnp.where(core == 0, w * 4 + x, x * 4 + w))
                grad = dot(jnp.concatenate(parts, axis=0), right).astype(bf16)
                for n, at in enumerate(places_):
                    out[at, STARTS[m] : STARTS[m] + rows, :] = grad[n * rows : (n + 1) * rows, :]


def closure_kernel(place, patches, field, m1, m2, m3, o1, o2, o3, out, act):
    core = place[0]
    cells = [(half, high) for half in range(2) for high in range(2)]
    first, middle, last = (m1, o1), (m2, o2), (m3, o3)
    rows = patches[...]
    for half, high in cells:
        pre = dot(rows, first[half][high])
        act[high * 2 + (core if half == 0 else 1 - core)] = (pre * logistic(pre)).astype(bf16)
    act_one = jnp.concatenate([act[r] for r in range(4)], axis=1)
    fix = jnp.zeros((64, 1536), f32)
    for half, high in cells:
        pre = dot(act_one, middle[half][high])
        fix = fix + dot_rows((pre * logistic(pre)).astype(bf16), last[half][high])
    fix = fix.astype(bf16).astype(f32)
    for i in range(2):
        for j in range(2):
            for g in range(12):
                row = (i * 2 + j) * 16
                tile = swap_blocks(fix[row : row + 16, g * 128 : g * 128 + 128])
                c, at = g // 4, i * 8 + (g % 4) * 2
                for a in range(2):
                    part = tile[a * 8 : a * 8 + 8, :]
                    here = (c, at + a, slice(j * 8, j * 8 + 8))
                    out[here] = field[here] + part


def total_of(refs, at):
    return sum(ref[at].astype(f32) for ref in refs)


def third_kernel(place, a, b, c, d, out):
    out[...] = total_of((a, b, c, d), slice(None)).astype(bf16)


def update_kernel(place, pieces, *refs):
    layers, moments, updated, momenta, fresh = refs[:3], refs[3:6], refs[6:9], refs[9:12], refs[12]
    cols = pl.ds(pl.multiple_of(place[4] * LANES, LANES), LANES)
    for m, (start, rows) in enumerate(zip(STARTS, ROWS)):
        grad = sum(pieces[n, start : start + rows, :].astype(f32) for n in range(16))
        momentum = momentum_keep * moments[m][:, cols] + grad
        new = layers[m][:, cols] - learn_rate * momentum
        momenta[m][...] = momentum
        updated[m][...] = new
        for copy in range(16):
            fresh[copy, start : start + rows, :] = new.astype(bf16)


def sum_plane(parts, place):
    got = spread(parts, 2)
    blocks = call(third_kernel, like((16, BLOCK, LANES), bf16), place, parts[0], *got)
    return exchange_planes(blocks)


def edges_of(field):
    rounded, found = field.astype(bf16), []
    for axis, dim in ((ROLE, 1), (BRICK, 2)):
        size, length = lax.axis_size(axis), field.shape[dim]
        up = [(i, (i + 1) % size) for i in range(size)]
        last = lax.slice_in_dim(rounded, length - 3, length, axis=dim)
        leading = lax.slice_in_dim(rounded, 0, 3, axis=dim)
        found.append(lax.ppermute(last, axis, up).astype(f32))
        found.append(lax.ppermute(leading, axis, [(b, a) for a, b in up]).astype(f32))
    return found


def blended(a, b, c, d, e):
    bend, tilt, floor = 13.0 / 12.0 / 64.0, 0.25 / 64.0, weno_eps / 64.0
    b0, b1, b2 = a - 2.0 * b + c, b - 2.0 * c + d, c - 2.0 * d + e
    t0, t1, t2 = a - 4.0 * b + 3.0 * c, b - d, 3.0 * c - 4.0 * d + e
    r0 = floor + bend * b0 * b0 + tilt * t0 * t0
    r1 = floor + bend * b1 * b1 + tilt * t1 * t1
    r2 = floor + bend * b2 * b2 + tilt * t2 * t2
    s0, s1, s2 = r0 * r0, r1 * r1, r2 * r2
    w0, w1, w2 = 0.1 * (s1 * s2), 0.6 * (s0 * s2), 0.3 * (s0 * s1)
    upper = w0 * (2.0 * a - 7.0 * b + 11.0 * c) + w1 * (5.0 * c + 2.0 * d - b) + w2 * (2.0 * c + 5.0 * d - e)
    return upper / (6.0 * (w0 + w1 + w2))


def face(plus, minus):
    return blended(*plus[0:5]) + blended(*minus[5:0:-1])


def advect_kernel(tops, field, low_x, high_x, low_y, high_y, out, top, plus_x, minus_x, rows, plus_y, minus_y, faces):
    speed = jnp.max(tops[...])

    def split(along, value):
        return 0.5 * (along * value + speed * value), 0.5 * (along * value - speed * value)

    def lay(at, planes):
        for c in range(3):
            plus_x[c, at], minus_x[c, at] = split(planes[0], planes[c])

    for n in range(3):
        lay(n, [low_x[c, n] for c in range(3)])
        lay(n + 19, [high_x[c, n] for c in range(3)])

    def inner(n, carry):
        lay(n + 3, [field[c, n] for c in range(3)])
        return carry

    lax.fori_loop(0, 16, inner, 0)
    factor = courant / speed
    top[...] = jnp.zeros((8, 128), f32)

    def face_x(c, n):
        return face([plus_x[c, n + k] for k in range(6)], [minus_x[c, n + k] for k in range(6)])

    def step(n, below):
        above = tuple(face_x(c, n + 1) for c in range(3))
        values = [field[c, n] for c in range(3)]
        for c in range(3):
            rows[c, 0:3, :] = low_y[c, n]
            rows[c, 3:19, :] = values[c]
            rows[c, 19:22, :] = high_y[c, n]
        for c in range(3):
            plus_y[...], minus_y[...] = split(rows[1], rows[c])
            faces[...] = face(
                [plus_y[k : k + 24, :] for k in range(6)], [minus_y[k : k + 24, :] for k in range(6)]
            )
            along_y = faces[1:17, :] - faces[0:16, :]
            plus, minus = split(values[2], values[c])
            shifts = (2, 1, 0, 127, 126, 125)
            edge = face(
                [pltpu.roll(plus, k, 1) if k else plus for k in shifts],
                [pltpu.roll(minus, k, 1) if k else minus for k in shifts],
            )
            along_z = edge - pltpu.roll(edge, 1, 1)
            new = values[c] - factor * ((above[c] - below[c]) + along_y + along_z)
            out[c, n] = new
            size = jnp.abs(new)
            top[...] = jnp.maximum(top[...], jnp.maximum(size[0:8, :], size[8:16, :]))
        return above

    lax.fori_loop(0, 16, step, tuple(face_x(c, 0) for c in range(3)))


def advect(tops, field, edges):
    planes, line = (3, 22, 16, 128), (32, 128)
    scratch = [pltpu.VMEM(planes, f32)] * 2 + [pltpu.VMEM((3, *line), f32)]
    scratch += [pltpu.VMEM(line, f32)] * 2 + [pltpu.VMEM((24, 128), f32)]
    return pl.pallas_call(
        advect_kernel,
        out_shape=(like(field.shape, f32), like((8, 128), f32)),
        in_specs=[VMEM] * 6,
        out_specs=(VMEM, VMEM),
        scratch_shapes=scratch,
        compiler_params=pltpu.CompilerParams(vmem_limit_bytes=8 << 20),
    )(tops, field, *edges)


def global_tops(top):
    other = swap_cores(top)
    top = jnp.maximum(top, other)
    for phase in range(3):
        others = spread(top, phase)
        for other in others:
            top = jnp.maximum(top, other)
    return top


def after(value, first):
    return lax.optimization_barrier((value, first))[0]


def one_step(current, top, first):
    tops = after(global_tops(top), first)
    edges = edges_of(current)
    return advect(tops, current, edges)


def whole(velocity, first, middle, last, first_moment, middle_moment, last_moment, patch_pick, targets):
    place = places()
    layers, moments = (first, middle, last), (first_moment, middle_moment, last_moment)
    copies = own_block(place, layers)
    square = exchange_planes(copies)
    mine, other = gather_matrices(square, place)
    top = call(top_kernel, like((8, 128), f32), place, velocity)
    patches, chosen = call(
        cut_kernel,
        (like((64, 1536), bf16), like((BLOCK, 1536), bf16)),
        place,
        velocity,
        patch_pick.reshape(BLOCK, 1),
    )
    chosen_other = swap_cores(chosen)
    between, top = one_step(velocity, top, mine[0])
    hold, share = call(
        forward_kernel,
        (like((BLOCK, 4096), bf16),) * 2,
        place,
        chosen,
        targets,
        *mine,
        *other,
        scratch=[
            pltpu.VMEM((4, BLOCK, LANES), bf16),
            pltpu.VMEM((4, BLOCK, LANES), f32),
            pltpu.VMEM((4, BLOCK, LANES), f32),
            pltpu.VMEM((4, BLOCK, LANES), bf16),
        ],
    )
    parts = call(
        gradient_kernel,
        (like((16, BLOCK, LANES), bf16),) * 4,
        place,
        hold,
        swap_cores(share),
        chosen,
        chosen_other,
        scratch=[pltpu.VMEM((32, rows, LANES), bf16) for rows in ROWS],
    )
    between, top = lax.optimization_barrier((between, top, parts[3]))[:2]
    pieces = sum_plane(parts, place)
    wide = tuple(like((rows, LANES), f32) for rows in ROWS)
    results = call(
        update_kernel,
        wide + wide + (like((16, BLOCK, LANES), bf16),),
        place,
        pieces,
        *layers,
        *moments,
    )
    mine, other = gather_matrices(exchange_planes(results[6]), place)
    current, _ = one_step(between, top, results[6])
    velocity_next = call(
        closure_kernel,
        like(velocity.shape, f32),
        place,
        patches,
        current,
        *mine,
        *other,
        scratch=[pltpu.VMEM((4, 64, LANES), bf16)],
    )
    return (velocity_next, *results[:6])


def solution(mesh):
    torus = Mesh(mesh.devices.reshape(SIZES), AXES)
    in_specs = (P(None, ROLE, BRICK, None),) + (P(BRICK, None),) * 6 + (P(AXES), P(AXES, None))
    out_specs = (P(None, ROLE, BRICK, None),) + (P(BRICK, ROLE),) * 6
    return jax.shard_map(whole, mesh=torus, in_specs=in_specs, out_specs=out_specs, check_vma=False)
```

```python
import math

import jax
import jax.numpy as jnp
from jax import lax
from jax.experimental import pallas as pl
from jax.experimental.pallas import tpu as pltpu
from jax.sharding import Mesh
from jax.sharding import PartitionSpec as P


AXES = ("role_0", "role_1", "brick_0", "brick_1", "brick_2")
SIZES = (2, 2, 4, 2, 4)
ROLE = ("role_0", "role_1")
BRICK = ("brick_0", "brick_1", "brick_2")
ROWS = (48, 32, 48)
STARTS = (0, 48, 80)
BLOCK = 128
LANES = 256


weno_eps = 1e-06
courant = 0.3
momentum_keep = 0.9
learn_rate = 0.3
bf16 = jnp.bfloat16
f32 = jnp.float32


def flat_id(x, y, z, c):
    return (((x // 2) * 2 + c) * 4 + y) * 8 + (x % 2) * 4 + z


def phase_pairs(phase, shift):
    pairs = []
    for c in range(2):
        dim = (0, 1, 2)[phase] if c == 0 else (2, 0, 1)[phase]
        for x in range(4):
            for y in range(4):
                for z in range(4):
                    to = [x, y, z]
                    to[dim] = (to[dim] + shift) % 4
                    pairs.append((flat_id(x, y, z, c), flat_id(*to, c)))
    return pairs


def planes():
    ring = range(4)
    groups = [[flat_id(x, y, z, 0) for y in ring for x in ring] for z in ring]
    return groups + [[flat_id(x, y, z, 1) for x in ring for z in ring] for y in ring]


def exchange_planes(blocks):
    return lax.all_to_all(blocks, AXES, 0, 0, tiled=True, axis_index_groups=planes())


def spread(parts, phase):
    take = (lambda s: parts[s]) if isinstance(parts, (list, tuple)) else (lambda s: parts)
    return [lax.ppermute(take(s), AXES, phase_pairs(phase, s)) for s in (1, 3, 2)]


def swap_cores(array):
    return lax.ppermute(array, "role_1", [(0, 1), (1, 0)])


def places():
    core = lax.axis_index("role_1")
    x = lax.axis_index("role_0") * 2 + lax.axis_index("brick_1")
    y = lax.axis_index("brick_0")
    z = lax.axis_index("brick_2")
    first = jnp.where(core == 0, x, z)
    second = jnp.where(core == 0, y, x)
    third = jnp.where(core == 0, z, y)
    role = lax.axis_index(ROLE)
    beside = jnp.where(core == 0, y, z)
    return jnp.stack([core, first, second, third, role, beside]).astype(jnp.int32)


VMEM = pl.BlockSpec(memory_space=pltpu.VMEM)
SMEM = pl.BlockSpec(memory_space=pltpu.SMEM)


def held(array):
    return math.prod(array.shape) * jnp.dtype(array.dtype).itemsize


def call(kernel, outs, place, *arrays, scratch=(), spare=4):
    room = sum(map(held, arrays)) + sum(map(held, jax.tree.leaves(outs))) + sum(map(held, scratch))
    return pl.pallas_call(
        kernel,
        out_shape=outs,
        in_specs=[SMEM] + [VMEM] * len(arrays),
        out_specs=jax.tree.map(lambda _: VMEM, outs),
        scratch_shapes=scratch,
        compiler_params=pltpu.CompilerParams(vmem_limit_bytes=room + (spare << 20)),
    )(place, *arrays)


def like(shape, dtype):
    return jax.ShapeDtypeStruct(shape, dtype)


def own_block_kernel(place, first, middle, last, out):
    for ref, start, rows in zip((first, middle, last), STARTS, ROWS):
        part = ref[...].astype(bf16)
        for copy in range(16):
            out[copy, start : start + rows, :] = part


def own_block(place, layers):
    grid = pltpu.PrefetchScalarGridSpec(
        num_scalar_prefetch=1,
        grid=(1,),
        in_specs=[pl.BlockSpec((rows, LANES), lambda i, place: (0, place[4])) for rows in ROWS],
        out_specs=pl.BlockSpec((16, BLOCK, LANES), lambda i, place: (0, 0, 0)),
    )
    return pl.pallas_call(
        own_block_kernel,
        out_shape=like((16, BLOCK, LANES), bf16),
        grid_spec=grid,
        compiler_params=pltpu.CompilerParams(vmem_limit_bytes=8 << 20),
        name="own_block",
    )(place, *layers)


def finish_kernel(of_other):
    def kernel(place, own, one, three, low, high_part, first, middle, last):
        core = 1 - place[0] if of_other else place[0]
        mine = place[5] if of_other else place[3]
        for s, ref in ((0, own), (1, one), (3, three), (2, None)):
            at3 = lax.rem(mine + 4 - s, 4)
            for at2 in range(4):
                for at1 in range(4):
                    n = at2 * 4 + at1
                    source, at = (ref, n) if ref is not None else ((low, n) if n < 8 else (high_part, n - 8))
                    x = jnp.where(core == 0, at1, at2)
                    y = jnp.where(core == 0, at2, at3)
                    z = jnp.where(core == 0, at3, at1)
                    high = x // 2
                    brick = y * 8 + (x - high * 2) * 4 + z
                    for out, start, rows in zip((first, middle, last), STARTS, ROWS):
                        to = pl.ds(pl.multiple_of(brick * rows, 16), rows)
                        out[high, to, :] = source[at, start : start + rows, :]

    return kernel


def gather_matrices(square, place):
    def shifted(array, shift):
        return lax.ppermute(array, AXES, phase_pairs(2, shift))

    def finish(pieces, of_other):
        return call(
            finish_kernel(of_other),
            tuple(like((2, 32 * rows, LANES), bf16) for rows in ROWS),
            place,
            *pieces,
        )

    one, three = shifted(square, 1), shifted(square, 3)
    given = [swap_cores(square)]
    low, high = shifted(one[:8], 1), shifted(three[8:], 3)
    given += [swap_cores(one), swap_cores(three)]
    given += [swap_cores(low), swap_cores(high)]
    mine = finish((square, one, three, low, high), False)
    return mine, finish(given, True)


def swap_blocks(tile):
    row = lax.broadcasted_iota(jnp.int32, (16, 128), 0)
    group = lax.broadcasted_iota(jnp.int32, (16, 128), 1) // 8
    for bit in (1, 2, 4, 8):
        row_set = (row & bit) != 0
        group_set = (group & bit) != 0
        down = pltpu.roll(pltpu.roll(tile, 16 - bit, 0), 8 * bit, 1)
        up = pltpu.roll(pltpu.roll(tile, bit, 0), 128 - 8 * bit, 1)
        moved = jnp.where(row_set, up, down)
        tile = jnp.where(row_set == group_set, tile, moved)
    return tile


def cut_kernel(place, field, pick, out, chosen):
    for i in range(2):
        for j in range(2):
            for g in range(12):
                c, at = g // 4, i * 8 + (g % 4) * 2
                low = field[c, at, j * 8 : j * 8 + 8, :]
                high = field[c, at + 1, j * 8 : j * 8 + 8, :]
                tile = swap_blocks(jnp.concatenate([low, high], axis=0))
                row = (i * 2 + j) * 16
                out[row : row + 16, g * 128 : g * 128 + 128] = tile.astype(bf16)
    which = lax.broadcasted_iota(jnp.int32, (BLOCK, 64), 1) == pick[...]
    chosen[...] = dot(which.astype(f32).astype(bf16), out[...]).astype(bf16)


def top_kernel(place, field, out):
    def take(n, top):
        return jnp.maximum(top, jnp.max(jnp.abs(field[n // 16, n % 16]).reshape(2, 8, 128), axis=0))

    out[...] = lax.fori_loop(0, 48, take, jnp.zeros((8, 128), f32))


def dot(a, b):
    return jnp.dot(a, b, preferred_element_type=f32)


def dot_rows(a, b):
    return lax.dot_general(a, b, (((1,), (1,)), ((), ())), preferred_element_type=f32)


def logistic(v):
    return 1.0 / (1.0 + jnp.exp(-v))


def forward_kernel(
    place, picked, targets, m1, m2, m3, o1, o2, o3, hold, share, act, slope_one, slope_two, act_two
):
    core = place[0]
    total = 128 * 128
    cells = [(half, high) for half in range(2) for high in range(2)]
    first, middle, last = (m1, o1), (m2, o2), (m3, o3)

    def role_of(half, high):
        return high * 2 + (core if half == 0 else 1 - core)

    chosen = picked[...]
    for half, high in cells:
        pre = dot(chosen, first[half][high])
        s = logistic(pre)
        r = role_of(half, high)
        act[r] = (pre * s).astype(bf16)
        slope_one[r] = s * (1.0 + pre * (1.0 - s))
    act_one = jnp.concatenate([act[r] for r in range(4)], axis=1)
    y = jnp.zeros((BLOCK, 1536), f32)
    for n, (half, high) in enumerate(cells):
        pre = dot(act_one, middle[half][high])
        s = logistic(pre)
        a = (pre * s).astype(bf16)
        act_two[n] = a
        slope_two[n] = s * (1.0 + pre * (1.0 - s))
        y = y + dot_rows(a, last[half][high])
    error = ((y - targets[...].astype(f32)) / total).astype(bf16)
    for out in (hold, share):
        out[:, 0:1536] = error
        out[:, 1536:2560] = act_one
    back_one = jnp.zeros((BLOCK, 1024), f32)
    for n, (half, high) in enumerate(cells):
        d = (dot(error, last[half][high]) * slope_two[n]).astype(bf16)
        out = share if half else hold
        out[:, 2560 + high * LANES : 2816 + high * LANES] = act_two[n]
        out[:, 3072 + high * LANES : 3328 + high * LANES] = d
        back_one = back_one + dot_rows(d, middle[half][high])
    for r in range(4):
        act[r] = (back_one[:, r * LANES : (r + 1) * LANES] * slope_one[r]).astype(bf16)
    for half, high in cells:
        out = share if half else hold
        out[:, 3584 + high * LANES : 3840 + high * LANES] = act[role_of(half, high)]


def gradient_kernel(
    place, hold, other, picked, picked_other, own, one, two, three, left_first, left_middle, left_last
):
    core, mine = place[0], place[3]

    def both(start, size):
        cols = slice(start, start + size)
        return jnp.concatenate([hold[:, cols], other[:, cols]], axis=0)

    def turned(v):
        return v.astype(f32).T.astype(bf16)

    jobs = (
        (2, left_last, both(0, 1536), 2560),
        (1, left_middle, both(1536, 1024), 3072),
        (0, left_first, jnp.concatenate([picked[...], picked_other[...]], axis=0), 3584),
    )
    for m, left, value, start in jobs:
        rows = ROWS[m]
        left[...] = turned(value).reshape(32, rows, LANES)
        for high in range(2):
            right = both(start + high * LANES, LANES)
            for s, out in enumerate((own, one, two, three)):
                at3 = lax.rem(mine + s, 4)
                parts, places_ = [], []
                for low in range(2):
                    for w in range(4):
                        x = high * 2 + low
                        brick = jnp.where(core == 0, w * 8 + at3, at3 * 8 + w) + low * 4
                        parts.append(left[brick])
                        places_.append(jnp.where(core == 0, w * 4 + x, x * 4 + w))
                grad = dot(jnp.concatenate(parts, axis=0), right).astype(bf16)
                for n, at in enumerate(places_):
                    out[at, STARTS[m] : STARTS[m] + rows, :] = grad[n * rows : (n + 1) * rows, :]


def closure_kernel(place, patches, field, m1, m2, m3, o1, o2, o3, out, act):
    core = place[0]
    cells = [(half, high) for half in range(2) for high in range(2)]
    first, middle, last = (m1, o1), (m2, o2), (m3, o3)
    rows = patches[...]
    for half, high in cells:
        pre = dot(rows, first[half][high])
        act[high * 2 + (core if half == 0 else 1 - core)] = (pre * logistic(pre)).astype(bf16)
    act_one = jnp.concatenate([act[r] for r in range(4)], axis=1)
    fix = jnp.zeros((64, 1536), f32)
    for half, high in cells:
        pre = dot(act_one, middle[half][high])
        fix = fix + dot_rows((pre * logistic(pre)).astype(bf16), last[half][high])
    fix = fix.astype(bf16).astype(f32)
    for i in range(2):
        for j in range(2):
            for g in range(12):
                row = (i * 2 + j) * 16
                tile = swap_blocks(fix[row : row + 16, g * 128 : g * 128 + 128])
                c, at = g // 4, i * 8 + (g % 4) * 2
                for a in range(2):
                    part = tile[a * 8 : a * 8 + 8, :]
                    here = (c, at + a, slice(j * 8, j * 8 + 8))
                    out[here] = field[here] + part


def total_of(refs, at):
    return sum(ref[at].astype(f32) for ref in refs)


def third_kernel(place, a, b, c, d, out):
    out[...] = total_of((a, b, c, d), slice(None)).astype(bf16)


def update_kernel(place, pieces, *refs):
    layers, moments, updated, momenta, fresh = refs[:3], refs[3:6], refs[6:9], refs[9:12], refs[12]
    cols = pl.ds(pl.multiple_of(place[4] * LANES, LANES), LANES)
    for m, (start, rows) in enumerate(zip(STARTS, ROWS)):
        grad = sum(pieces[n, start : start + rows, :].astype(f32) for n in range(16))
        momentum = momentum_keep * moments[m][:, cols] + grad
        new = layers[m][:, cols] - learn_rate * momentum
        momenta[m][...] = momentum
        updated[m][...] = new
        for copy in range(16):
            fresh[copy, start : start + rows, :] = new.astype(bf16)


def sum_plane(parts, place):
    got = spread(parts, 2)
    blocks = call(third_kernel, like((16, BLOCK, LANES), bf16), place, parts[0], *got)
    return exchange_planes(blocks)


def edges_of(field):
    rounded, found = field.astype(bf16), []
    for axis, dim in ((ROLE, 1), (BRICK, 2)):
        size, length = lax.axis_size(axis), field.shape[dim]
        up = [(i, (i + 1) % size) for i in range(size)]
        last = lax.slice_in_dim(rounded, length - 3, length, axis=dim)
        leading = lax.slice_in_dim(rounded, 0, 3, axis=dim)
        found.append(lax.ppermute(last, axis, up))
        found.append(lax.ppermute(leading, axis, [(b, a) for a, b in up]))
    return found


def blended(a, b, c, d, e):
    bend, tilt, floor = 13.0 / 12.0 / 64.0, 0.25 / 64.0, weno_eps / 64.0
    b0, b1, b2 = a - 2.0 * b + c, b - 2.0 * c + d, c - 2.0 * d + e
    t0, t1, t2 = a - 4.0 * b + 3.0 * c, b - d, 3.0 * c - 4.0 * d + e
    r0 = floor + bend * b0 * b0 + tilt * t0 * t0
    r1 = floor + bend * b1 * b1 + tilt * t1 * t1
    r2 = floor + bend * b2 * b2 + tilt * t2 * t2
    s0, s1, s2 = r0 * r0, r1 * r1, r2 * r2
    w0, w1, w2 = 0.1 * (s1 * s2), 0.6 * (s0 * s2), 0.3 * (s0 * s1)
    upper = w0 * (2.0 * a - 7.0 * b + 11.0 * c) + w1 * (5.0 * c + 2.0 * d - b) + w2 * (2.0 * c + 5.0 * d - e)
    return upper / (6.0 * (w0 + w1 + w2))


def face(plus, minus):
    return blended(*plus[0:5]) + blended(*minus[5:0:-1])


def advect_kernel(tops, field, low_x, high_x, low_y, high_y, out, top, plus_x, minus_x, rows, plus_y, minus_y, faces):
    speed = jnp.max(tops[...])

    def split(along, value):
        return 0.5 * (along * value + speed * value), 0.5 * (along * value - speed * value)

    def lay(at, planes):
        for c in range(3):
            plus_x[c, at], minus_x[c, at] = split(planes[0], planes[c])

    for n in range(3):
        lay(n, [low_x[c, n] for c in range(3)])
        lay(n + 19, [high_x[c, n] for c in range(3)])

    def inner(n, carry):
        lay(n + 3, [field[c, n] for c in range(3)])
        return carry

    lax.fori_loop(0, 16, inner, 0)
    factor = courant / speed
    top[...] = jnp.zeros((8, 128), f32)

    def face_x(c, n):
        return face([plus_x[c, n + k] for k in range(6)], [minus_x[c, n + k] for k in range(6)])

    def step(n, below):
        above = tuple(face_x(c, n + 1) for c in range(3))
        values = [field[c, n] for c in range(3)]
        for c in range(3):
            rows[c, 0:3, :] = low_y[c, n]
            rows[c, 3:19, :] = values[c]
            rows[c, 19:22, :] = high_y[c, n]
        for c in range(3):
            plus_y[...], minus_y[...] = split(rows[1], rows[c])
            faces[...] = face(
                [plus_y[k : k + 24, :] for k in range(6)], [minus_y[k : k + 24, :] for k in range(6)]
            )
            along_y = faces[1:17, :] - faces[0:16, :]
            plus, minus = split(values[2], values[c])
            shifts = (2, 1, 0, 127, 126, 125)
            edge = face(
                [pltpu.roll(plus, k, 1) if k else plus for k in shifts],
                [pltpu.roll(minus, k, 1) if k else minus for k in shifts],
            )
            along_z = edge - pltpu.roll(edge, 1, 1)
            new = values[c] - factor * ((above[c] - below[c]) + along_y + along_z)
            out[c, n] = new
            size = jnp.abs(new)
            top[...] = jnp.maximum(top[...], jnp.maximum(size[0:8, :], size[8:16, :]))
        return above

    lax.fori_loop(0, 16, step, tuple(face_x(c, 0) for c in range(3)))


def advect(tops, field, edges):
    planes, line = (3, 22, 16, 128), (32, 128)
    scratch = [pltpu.VMEM(planes, f32)] * 2 + [pltpu.VMEM((3, *line), f32)]
    scratch += [pltpu.VMEM(line, f32)] * 2 + [pltpu.VMEM((24, 128), f32)]
    return pl.pallas_call(
        advect_kernel,
        out_shape=(like(field.shape, f32), like((8, 128), f32)),
        in_specs=[VMEM] * 6,
        out_specs=(VMEM, VMEM),
        scratch_shapes=scratch,
        compiler_params=pltpu.CompilerParams(vmem_limit_bytes=8 << 20),
    )(tops, field, *edges)


def global_tops(top):
    other = swap_cores(top)
    top = jnp.maximum(top, other)
    for phase in range(3):
        others = spread(top, phase)
        for other in others:
            top = jnp.maximum(top, other)
    return top


def after(value, first):
    return lax.optimization_barrier((value, first))[0]


def one_step(current, top, first):
    tops = after(global_tops(top), first)
    edges = edges_of(current)
    edges = [edge.astype(f32) for edge in edges]
    return advect(tops, current, edges)


def whole(velocity, first, middle, last, first_moment, middle_moment, last_moment, patch_pick, targets):
    place = places()
    layers, moments = (first, middle, last), (first_moment, middle_moment, last_moment)
    copies = own_block(place, layers)
    square = exchange_planes(copies)
    mine, other = gather_matrices(square, place)
    top = call(top_kernel, like((8, 128), f32), place, velocity)
    patches, chosen = call(
        cut_kernel,
        (like((64, 1536), bf16), like((BLOCK, 1536), bf16)),
        place,
        velocity,
        patch_pick.reshape(BLOCK, 1),
    )
    chosen_other = swap_cores(chosen)
    between, top = one_step(velocity, top, mine[0])
    hold, share = call(
        forward_kernel,
        (like((BLOCK, 4096), bf16),) * 2,
        place,
        chosen,
        targets,
        *mine,
        *other,
        scratch=[
            pltpu.VMEM((4, BLOCK, LANES), bf16),
            pltpu.VMEM((4, BLOCK, LANES), f32),
            pltpu.VMEM((4, BLOCK, LANES), f32),
            pltpu.VMEM((4, BLOCK, LANES), bf16),
        ],
    )
    parts = call(
        gradient_kernel,
        (like((16, BLOCK, LANES), bf16),) * 4,
        place,
        hold,
        swap_cores(share),
        chosen,
        chosen_other,
        scratch=[pltpu.VMEM((32, rows, LANES), bf16) for rows in ROWS],
    )
    between, top = lax.optimization_barrier((between, top, parts[3]))[:2]
    pieces = sum_plane(parts, place)
    wide = tuple(like((rows, LANES), f32) for rows in ROWS)
    results = call(
        update_kernel,
        wide + wide + (like((16, BLOCK, LANES), bf16),),
        place,
        pieces,
        *layers,
        *moments,
    )
    mine, other = gather_matrices(exchange_planes(results[6]), place)
    current, _ = one_step(between, top, results[6])
    velocity_next = call(
        closure_kernel,
        like(velocity.shape, f32),
        place,
        patches,
        current,
        *mine,
        *other,
        scratch=[pltpu.VMEM((4, 64, LANES), bf16)],
    )
    return (velocity_next, *results[:6])


def solution(mesh):
    torus = Mesh(mesh.devices.reshape(SIZES), AXES)
    in_specs = (P(None, ROLE, BRICK, None),) + (P(BRICK, None),) * 6 + (P(AXES), P(AXES, None))
    out_specs = (P(None, ROLE, BRICK, None),) + (P(BRICK, ROLE),) * 6
    return jax.shard_map(whole, mesh=torus, in_specs=in_specs, out_specs=out_specs, check_vma=False)
```
